32 devices in a mesh: group: 1, wide: 32 (over z, y, x, core).
Axes of the slice: x: 2, y: 2, z: 4, core: 2. Of those that a mesh axis runs over, the one named last changes fastest.
Arguments:
- resid: bfloat16 [32, 3072], P(('group', 'wide')), may hold values from -6 to 6
- query: bfloat16 [32, 4096], P(('group', 'wide')), may hold values from -4 to 4
- key: bfloat16 [32, 4096], P(('group', 'wide')), may hold values from -4 to 4
- value: bfloat16 [32, 4096], P(('group', 'wide')), may hold values from -6 to 6
- state: float32 [32, 32, 128, 128], P(('group', 'wide')), may hold values from -6 to 6
- decay: float32 [32], replicated, may hold values from 0.02 to 2
- out_gate: bfloat16 [32, 4096], P(('group', 'wide')), may hold values from -6 to 6
- norm_gain: float32 [4096], replicated, may hold values from 0.25 to 1.75
- w_out: bfloat16 [4096, 3072], P('wide'), may hold values from -0.09375 to 0.09375
- moe_gain: float32 [3072], replicated, may hold values from 0.25 to 1.75
- w_gate: bfloat16 [32, 576, 3072], P('wide'), may hold values from -0.109375 to 0.109375
- w_up: bfloat16 [32, 576, 3072], P('wide'), may hold values from -0.109375 to 0.109375
- w_down: bfloat16 [32, 576, 3072], P('wide'), may hold values from -0.09375 to 0.09375
- expert_ids: int32 [32, 2], P('group'), may hold values from 0 to 3, all different within a row; in each aligned block of 32 rows (0 to 31, 32 to 63, ...) at most 32 rows name the same one
- expert_weights: float32 [32, 2], P('group'), may hold values from 0.2 to 1
Outputs:
- mixed: bfloat16 [32, 3072], P(('group', 'wide'))
The draws below stay inside these ranges and needn't reach their ends.
Inputs may be any that keep to these rules, and one draw needn't show every extreme that they name: `expert_ids`: each request names two different experts; every expert is named by some request; no expert is named by more than 32 requests, a bound that some block reaches.
All inputs are finite; a program needn't handle non-finite values.
Results may differ from the reference program's by a relative error of at most 0.012.
Values may be sent and summed in bfloat16 or wider, within the bound.
No kernel may reach another device: no remote copies, remote signals or barrier semaphores. Data moves between devices by JAX's collectives and lax.ppermute only.
A program may use at most 64 MiB of HBM per device.

```python
import math
import jax
import jax.numpy as jnp
import numpy as np
from jax import lax

D = 3072
HEADS = 32
HDIM = 128
FF = 4608
SPLIT = 8
ROWS = 32
EXPERTS = 4
CAP = 32
FF_DEV = 576
ATT = 4096


def block_scale(key, shape, pieces, smallest, top_value):
    def one(axis_at, shards_of):
        heights = jax.random.uniform(jax.random.fold_in(jax.random.fold_in(key, 6), axis_at), (shards_of,), jnp.float32, smallest / len(pieces), top_value / len(pieces))
        return jnp.repeat(jnp.exp(heights), shape[axis_at] // shards_of).reshape((-1,) + (1,) * (len(shape) - axis_at - 1))

    level = one(*pieces[0])
    for cut in pieces[1:]:
        level = level * one(*cut)
    return level


def assign_block(rng, own, number, rows, amount, top, reach, skew):
    order = jax.random.permutation(rng, amount)
    packed, common = shares(amount, rows * top, reach, skew, True), shares(amount, rows * top, reach, skew, False)
    places = jnp.arange(amount)

    def named(lengths, turn):
        used = int((lengths > 0).sum())
        fixed = max(1, used // 4)
        moved = fixed + (places - fixed + turn * (used - fixed)) % max(1, amount - fixed)
        return jnp.zeros((amount,), jnp.int32).at[order[jnp.where(places < fixed, places, moved)]].set(jnp.asarray(lengths, jnp.int32))

    lengths = jnp.where(number % 4 == 0, named(packed, number // 4), named(common, number - number // 4 - 1))
    mixed = jax.random.permutation(jax.random.fold_in(own, 3), amount)
    donor, taker = mixed[0:amount // 2 * 2:2], mixed[1:amount // 2 * 2:2]
    margin = jnp.minimum(lengths[donor] - 1, reach - lengths[taker]) // 2
    margin = jnp.where((donor == order[0]) | (taker == order[0]) | (lengths[taker] == 0), 0, jnp.maximum(margin, 0))
    moved = jax.random.randint(jax.random.fold_in(own, 4), (amount // 2,), 0, 1 << 20) % (margin + 1)
    lengths = lengths.at[donor].add(-moved).at[taker].add(moved)
    items = jnp.searchsorted(jnp.cumsum(lengths), jnp.arange(rows * top), side="right").astype(jnp.int32)
    table = items.reshape(top, rows).T
    table = table[jax.random.permutation(jax.random.fold_in(own, 1), rows)]
    turn = jax.random.randint(jax.random.fold_in(own, 2), (rows, 1), 0, top)
    return jnp.take_along_axis(table, (jnp.arange(top)[None, :] + turn) % top, axis=1)


def shares(amount, total, limit, lean, full):
    weights = [(1 << 20) // math.isqrt(grade ** lean) + 1 for grade in range(1, amount + 1)]
    largest = limit if full else min(limit, max(-(-total // amount), total * weights[0] // sum(weights)))
    least = 1 if total - largest >= amount - 1 else 0
    holding, spare = [largest] + [least] * (amount - 1), total - largest - least * (amount - 1)
    while spare > 0:
        candidates = [i for i in range(1, amount) if holding[i] < largest] or [i for i in range(1, amount) if holding[i] < limit]
        mass, left = sum([weights[i] for i in candidates]), spare
        for i in candidates:
            more = min(limit - holding[i], max(1, left * weights[i] // mass), spare)
            holding[i] = holding[i] + more
            spare = spare - more
    return np.array(holding)


def noise(own_key, extent, scale, reach, shards=(), held_as=jnp.bfloat16):
    entries = scale * jax.random.normal(own_key, extent, jnp.float32)
    if shards:
        entries = entries * block_scale(own_key, extent, shards, -0.22, 0.18)
    return jnp.clip(entries, -reach, reach).astype(held_as)


def setup_inputs(seed: int = 0, part: int = 0) -> dict:
    seeds = jax.random.split(jax.random.key(seed), 16)
    part_splits = jax.random.split(jax.random.fold_in(seeds[15], part), 16)
    resid = noise(part_splits[0], (ROWS, D), 1.0, 6.0, ((0, 32),))
    query = noise(part_splits[1], (ROWS, ATT), 0.3, 4.0, ((0, 32),))
    key = noise(part_splits[2], (ROWS, ATT), 0.3, 4.0, ((0, 32),))
    value = noise(part_splits[3], (ROWS, ATT), 1.0, 6.0, ((0, 32),))
    state = noise(part_splits[4], (ROWS, HEADS, HDIM, HDIM), 0.5, 6.0, ((0, 32),), jnp.float32)
    decay = jnp.clip(jnp.exp(jax.random.uniform(seeds[5], (HEADS,), jnp.float32, math.log(0.02), math.log(2.0))), 0.02, 2.0)
    out_gate = noise(part_splits[6], (ROWS, ATT), 1.0, 6.0, ((0, 32),))
    norm_gain = jnp.clip(1.0 + 0.15 * jax.random.normal(seeds[7], (ATT,), jnp.float32), 0.25, 1.75)
    w_out = noise(seeds[8], (ATT, D), ATT ** -0.5, 0.09375, ((0, 32),))
    moe_gain = jnp.clip(1.0 + 0.15 * jax.random.normal(seeds[9], (D,), jnp.float32), 0.25, 1.75)
    w_gate = noise(seeds[10], (EXPERTS * SPLIT, FF_DEV, D), D ** -0.5, 0.109375, ((0, 32),))
    w_up = noise(seeds[11], (EXPERTS * SPLIT, FF_DEV, D), D ** -0.5, 0.109375, ((0, 32),))
    w_down = noise(seeds[12], (EXPERTS * SPLIT, FF_DEV, D), FF ** -0.5, 0.09375, ((0, 32),))
    expert_ids_keys = jax.random.split(jax.random.fold_in(part_splits[13], 1), ROWS // ROWS)
    expert_ids_turns = jax.random.permutation(jax.random.fold_in(part_splits[13], 3), ROWS // ROWS)
    expert_ids = jax.vmap(lambda own, number: assign_block(jax.random.fold_in(part_splits[13], 2), own, number, ROWS, EXPERTS, 2, CAP, 2))(expert_ids_keys, expert_ids_turns).reshape((ROWS, 2))
    expert_weights = jnp.clip(jax.random.uniform(part_splits[14], (ROWS, 2), jnp.float32, 0.2, 1.0), 0.2, 1.0)
    return {"resid": resid, "query": query, "key": key, "value": value, "state": state, "decay": decay, "out_gate": out_gate, "norm_gain": norm_gain, "w_out": w_out, "moe_gain": moe_gain, "w_gate": w_gate, "w_up": w_up, "w_down": w_down, "expert_ids": expert_ids, "expert_weights": expert_weights}


def by_rows(left, weight):
    return lax.dot_general(left, weight, (((1,), (1,)), ((), ())), preferred_element_type=jnp.float32)

def reference(resid, query, key, value, state, decay, out_gate, norm_gain, w_out, moe_gain, w_gate, w_up, w_down, expert_ids, expert_weights):
    rows = resid.shape[0]
    q_heads = query.astype(jnp.float32).reshape(rows, HEADS, HDIM)
    k_heads = key.astype(jnp.float32).reshape(rows, HEADS, HDIM)
    v_heads = value.astype(jnp.float32).reshape(rows, HEADS, HDIM)
    fade = jnp.exp(-decay)
    new_state = fade[None, :, None, None] * state + jnp.einsum('rhi,rhj->rhij', k_heads, v_heads)
    att = jnp.einsum('rhi,rhij->rhj', q_heads, new_state).reshape(rows, HEADS * HDIM)
    scale = lax.rsqrt(lax.optimization_barrier(jnp.mean(att * att, axis=1, keepdims=True)) + 1e-06)
    attn = (att * scale * norm_gain * jax.nn.sigmoid(out_gate.astype(jnp.float32))).astype(jnp.bfloat16)
    proj = jnp.dot(attn, w_out, preferred_element_type=jnp.float32)
    hid_res = (resid.astype(jnp.float32) + proj).astype(jnp.bfloat16)
    hid_f = hid_res.astype(jnp.float32)
    normed = (hid_f * lax.rsqrt(lax.optimization_barrier(jnp.mean(hid_f * hid_f, axis=1, keepdims=True)) + 1e-06) * moe_gain).astype(jnp.bfloat16)
    experts = jnp.arange(EXPERTS, dtype=jnp.int32)
    coef = lax.optimization_barrier(jnp.sum(jnp.where(expert_ids[:, :, None] == experts[None, None, :], expert_weights[:, :, None], 0.0), axis=1))
    slabs = jnp.arange(EXPERTS * SPLIT, dtype=jnp.int32)

    def one_slab(total, inputs):
        gate_w, up_w, down_w, slab = inputs
        gate = by_rows(normed, gate_w)
        upper = by_rows(normed, up_w)
        inner = (jax.nn.silu(gate) * upper).astype(jnp.bfloat16)
        weight = lax.optimization_barrier(jnp.sum(jnp.where(experts[None, :] == slab // SPLIT, coef, 0.0), axis=1))
        part = jnp.dot(inner, down_w, preferred_element_type=jnp.float32) * weight[:, None]
        return (total + part, None)
    total, _ = lax.scan(one_slab, jnp.zeros((rows, D), jnp.float32), (w_gate, w_up, w_down, slabs))
    return (hid_f + total).astype(jnp.bfloat16)
```

```python
import jax
import jax.numpy as jnp
from jax import lax
from jax.sharding import PartitionSpec as P

SPLIT = 8


def by_rows(left, weight):
    return lax.dot_general(
        left, weight, (((1,), (1,)), ((), ())), preferred_element_type=jnp.float32
    )


def exchange(blocks):
    return lax.all_to_all(blocks, "wide", split_axis=0, concat_axis=0, tiled=True)


def shards(
    resid,
    query,
    key,
    value,
    state,
    decay,
    out_gate,
    norm_gain,
    w_out,
    moe_gain,
    w_gate,
    w_up,
    w_down,
    expert_ids,
    expert_weights,
):
    local_rows, width = resid.shape
    heads = decay.shape[0]
    head_size = query.shape[1] // heads
    devices = lax.axis_size("wide")
    rows = devices * local_rows
    q_heads = query.astype(jnp.float32).reshape(local_rows, heads, head_size)
    k_heads = key.astype(jnp.float32).reshape(local_rows, heads, head_size)
    v_heads = value.astype(jnp.float32).reshape(local_rows, heads, head_size)
    fade = jnp.exp(-decay)
    new_state = fade[None, :, None, None] * state + jnp.einsum("rhi,rhj->rhij", k_heads, v_heads)
    att = jnp.einsum("rhi,rhij->rhj", q_heads, new_state).reshape(local_rows, heads * head_size)
    scale = lax.rsqrt(jnp.mean(att * att, axis=1, keepdims=True) + 1e-06)
    attn = (att * scale * norm_gain * jax.nn.sigmoid(out_gate.astype(jnp.float32))).astype(
        jnp.bfloat16
    )
    columns = lax.all_to_all(attn, "wide", split_axis=1, concat_axis=0, tiled=True)
    proj = jnp.dot(columns, w_out, preferred_element_type=jnp.float32).astype(jnp.bfloat16)
    parts = exchange(proj.reshape(devices, local_rows, width))
    summed = jnp.sum(parts.astype(jnp.float32), axis=0)
    hid_res = (resid.astype(jnp.float32) + summed).astype(jnp.bfloat16)
    hid_f = hid_res.astype(jnp.float32)
    normed = (
        hid_f * lax.rsqrt(jnp.mean(hid_f * hid_f, axis=1, keepdims=True) + 1e-06) * moe_gain
    ).astype(jnp.bfloat16)
    all_inputs = exchange(jnp.broadcast_to(normed[None], (devices, local_rows, width)))
    all_inputs = all_inputs.reshape(rows, width)
    owner = lax.axis_index("wide") // SPLIT
    weight_all = jnp.sum(jnp.where(expert_ids == owner, expert_weights, 0.0), axis=1)
    gate = by_rows(all_inputs, w_gate[0])
    upper = by_rows(all_inputs, w_up[0])
    inner = (jax.nn.silu(gate) * upper).astype(jnp.bfloat16)
    partial_value = jnp.dot(inner, w_down[0], preferred_element_type=jnp.float32)
    partial_value = (partial_value * weight_all[:, None]).astype(jnp.bfloat16)
    returned = exchange(partial_value.reshape(devices, local_rows, width))
    experts_out = jnp.sum(returned.astype(jnp.float32), axis=0)
    return (hid_f + experts_out).astype(jnp.bfloat16)


def solution(mesh):
    return jax.shard_map(
        shards,
        mesh=mesh,
        in_specs=(
            P(("group", "wide"), None),
            P(("group", "wide"), None),
            P(("group", "wide"), None),
            P(("group", "wide"), None),
            P(("group", "wide"), None, None, None),
            P(),
            P(("group", "wide"), None),
            P(),
            P("wide", None),
            P(),
            P("wide", None, None),
            P("wide", None, None),
            P("wide", None, None),
            P("group", None),
            P("group", None),
        ),
        out_specs=P(("group", "wide"), None),
        check_vma=False,
    )
```

```python
import functools

import jax
import jax.numpy as jnp
from jax import lax
from jax.experimental import pallas as pl
from jax.experimental.pallas import tpu as pltpu
from jax.sharding import PartitionSpec as P

SPLIT = 8
LANES = 128
HEAD_BLOCKS = 4
WEIGHT_BLOCKS = 4
VMEM = pl.BlockSpec(memory_space=pltpu.VMEM)
HBM = pl.BlockSpec(memory_space=pltpu.HBM)
MIB = 1024 * 1024


def off_chip(*values):
    return [pltpu.with_memory_space_constraint(value, pltpu.HBM) for value in values]


def on_chip(*values):
    return [pltpu.with_memory_space_constraint(value, pltpu.VMEM) for value in values]


def call(body, out_shape, in_specs, scratch, flops, moved, limit):
    return pl.pallas_call(
        body,
        out_shape=out_shape,
        in_specs=in_specs,
        out_specs=jax.tree.map(lambda _: VMEM, out_shape),
        scratch_shapes=scratch,
        compiler_params=pltpu.CompilerParams(vmem_limit_bytes=limit),
        cost_estimate=pl.CostEstimate(flops=flops, bytes_accessed=moved, transcendentals=0),
    )


def exchange(blocks):
    return lax.all_to_all(blocks, "wide", split_axis=0, concat_axis=0, tiled=True)


def unfold(row_ref, held):
    for at in range(held.shape[0]):
        held[at : at + 1, :] = row_ref[0:1, at * LANES : (at + 1) * LANES].astype(jnp.float32)


def attention(
    query_ref, key_ref, value_ref, gate_ref, norm_ref, decay_ref, state_ref, resid_ref,
    moe_ref, ids_ref, weights_ref, w_out_ref, w_gate_ref,
    out_ref, resid_out, moe_out, coef_ref, w_out_copy, w_gate_copy,
    rows, norm_held, decay_held, states, resid_held, ids_held, weights_held,
    q_held, k_held, v_held, g_held, att, sems,
):
    heads = decay_held.shape[0]
    block = heads // HEAD_BLOCKS
    started = []

    def fetch(source, target):
        copy = pltpu.make_async_copy(source, target, sems.at[len(started)])
        copy.start()
        started.append(copy)
        return copy

    small = [fetch(ref, rows.at[at]) for at, ref in enumerate((query_ref, key_ref))]
    small.append(fetch(decay_ref, decay_held))
    parts = [pl.ds(at * block, block) for at in range(HEAD_BLOCKS)]
    read = [fetch(state_ref.at[0, part], states.at[part]) for part in parts]
    later = [fetch(ref, rows.at[2 + at]) for at, ref in enumerate((value_ref, gate_ref))]
    later.append(fetch(norm_ref, norm_held))
    later.append(fetch(resid_ref, resid_held))
    later.append(fetch(ids_ref, ids_held))
    later.append(fetch(weights_ref, weights_held))
    last = [fetch(moe_ref, moe_out), fetch(w_out_ref, w_out_copy), fetch(w_gate_ref, w_gate_copy)]

    for copy in small:
        copy.wait()
    unfold(rows.at[0], q_held)
    unfold(rows.at[1], k_held)
    q_rows = q_held[...]
    q_columns = q_rows.T
    both = jnp.sum(q_rows * k_held[...], axis=1, keepdims=True)
    for at in range(HEAD_BLOCKS):
        read[at].wait()
        for head in range(at * block, (at + 1) * block):
            seen = jnp.sum(q_columns[:, head : head + 1] * states[head], axis=0, keepdims=True)
            fade = jnp.exp(jnp.full((1, LANES), -decay_held[head], jnp.float32))
            att[head : head + 1, :] = fade * seen
    for copy in later:
        copy.wait()
    unfold(rows.at[2], v_held)
    unfold(rows.at[3], g_held)
    found = att[...] + both * v_held[...]
    scale = lax.rsqrt(jnp.sum(found * found, keepdims=True) / found.size + 1e-06)
    out_ref[...] = found * scale * norm_held[...] * jax.nn.sigmoid(g_held[...])

    unfold(resid_held, resid_out)
    owner = lax.axis_index("wide") // SPLIT
    named = jnp.where(ids_held[...] == owner, weights_held[...], 0.0)
    along = jnp.sum(named, axis=0, keepdims=True)
    square = (coef_ref.shape[0], coef_ref.shape[0])
    same = lax.broadcasted_iota(jnp.int32, square, 0) == lax.broadcasted_iota(jnp.int32, square, 1)
    column = jnp.sum(jnp.where(same, along, 0.0), axis=1, keepdims=True)
    coef_ref[...] = jnp.broadcast_to(column, coef_ref.shape)
    for copy in last:
        copy.wait()


def rows_to_blocks(spread, out_ref):
    rows, tiles, _ = out_ref.shape
    for row in range(rows):
        out_ref[row] = spread[pl.ds(row * tiles, tiles), :].astype(out_ref.dtype)


def project(columns_ref, w_ref, out_ref, spread):
    rows, tiles, _ = out_ref.shape
    made = jnp.dot(
        columns_ref[...].astype(jnp.bfloat16), w_ref[...], preferred_element_type=jnp.float32
    )
    for tile in range(tiles):
        spread[pl.ds(tile, rows, stride=tiles), :] = made[:, tile * LANES : (tile + 1) * LANES]
    rows_to_blocks(spread, out_ref)


def add_up(parts_ref):
    total = parts_ref[0].astype(jnp.float32)
    for at in range(1, parts_ref.shape[0]):
        total = total + parts_ref[at].astype(jnp.float32)
    return total


def middle(parts_ref, resid_ref, gain_ref, hid_ref, copies_ref):
    hid = (resid_ref[...] + add_up(parts_ref)).astype(jnp.bfloat16).astype(jnp.float32)
    hid_ref[...] = hid
    scale = lax.rsqrt(jnp.sum(hid * hid, keepdims=True) / hid.size + 1e-06)
    normed = (hid * scale * gain_ref[...]).astype(jnp.bfloat16)
    for at in range(copies_ref.shape[0]):
        copies_ref[at] = normed


def experts(
    blocks_ref, coef_ref, gate_ref, up_ref, down_ref, out_ref, spread, inputs, up, down, sems
):
    rows, tiles, _ = out_ref.shape
    hidden = gate_ref.shape[0]
    block = hidden // WEIGHT_BLOCKS
    parts = [pl.ds(at * block, block) for at in range(WEIGHT_BLOCKS)]
    copies = []
    for source, target in ((up_ref, up), (down_ref, down)):
        for part in parts:
            copy = pltpu.make_async_copy(source.at[0, part], target.at[part], sems.at[len(copies)])
            copy.start()
            copies.append(copy)
    for row in range(rows):
        spread[pl.ds(row * tiles, tiles), :] = blocks_ref[row].astype(jnp.float32)
    for tile in range(tiles):
        inputs[:, tile * LANES : (tile + 1) * LANES] = spread[
            pl.ds(tile, rows, stride=tiles), :
        ].astype(jnp.bfloat16)
    given = inputs[...]
    by_rows = functools.partial(
        lax.dot_general,
        dimension_numbers=(((1,), (1,)), ((), ())),
        preferred_element_type=jnp.float32,
    )
    gate = jax.nn.silu(by_rows(given, gate_ref[...]))
    for copy in copies[:WEIGHT_BLOCKS]:
        copy.wait()
    inner = (gate * by_rows(given, up[...])).astype(jnp.bfloat16)
    for copy in copies[WEIGHT_BLOCKS:]:
        copy.wait()
    made = jnp.dot(inner, down[...], preferred_element_type=jnp.float32)
    coef = coef_ref[...]
    for tile in range(tiles):
        spread[pl.ds(tile, rows, stride=tiles), :] = (
            made[:, tile * LANES : (tile + 1) * LANES] * coef
        )
    rows_to_blocks(spread, out_ref)


def finish(parts_ref, hid_ref, out_ref):
    mixed = hid_ref[...] + add_up(parts_ref)
    for at in range(mixed.shape[0]):
        out_ref[0:1, at * LANES : (at + 1) * LANES] = mixed[at : at + 1, :].astype(out_ref.dtype)


def shards(
    resid,
    query,
    key,
    value,
    state,
    decay,
    out_gate,
    norm_gain,
    w_out,
    moe_gain,
    w_gate,
    w_up,
    w_down,
    expert_ids,
    expert_weights,
):
    width = resid.shape[1]
    heads = decay.shape[0]
    features = query.shape[1]
    devices = lax.axis_size("wide")
    tiles = width // LANES
    hidden = w_gate.shape[1]
    f32, bf16 = jnp.float32, jnp.bfloat16
    row = pltpu.VMEM((tiles, LANES), f32)
    blocks = pltpu.VMEM((devices, tiles, LANES), bf16)
    spread = pltpu.VMEM((devices * tiles, LANES), f32)
    per_head = pltpu.VMEM((heads, LANES), f32)

    attn, resid_rows, moe_rows, coef, w_out_held, w_gate_held = call(
        attention,
        (
            per_head,
            row,
            row,
            pltpu.VMEM((devices, LANES), f32),
            pltpu.VMEM(w_out.shape, bf16),
            pltpu.VMEM(w_gate.shape[1:], bf16),
        ),
        [HBM] * 13,
        [
            pltpu.VMEM((4, 1, features), bf16),
            per_head,
            pltpu.SMEM((heads,), f32),
            pltpu.VMEM(state.shape[1:], f32),
            pltpu.VMEM((1, width), bf16),
            pltpu.VMEM((2, devices), jnp.int32),
            pltpu.VMEM((2, devices), f32),
        ]
        + [per_head] * 5
        + [pltpu.SemaphoreType.DMA((12 + HEAD_BLOCKS,))],
        2 * state.size,
        4 * state.size,
        8 * MIB,
    )(
        *off_chip(
            query,
            key,
            value,
            out_gate,
            norm_gain.reshape(heads, LANES),
            decay,
            state,
            resid,
            moe_gain.reshape(tiles, LANES),
            expert_ids.T,
            expert_weights.T,
            w_out,
            w_gate.reshape(w_gate.shape[1:]),
        )
    )
    columns = exchange(attn.reshape(devices, 1, features // devices))
    parts = call(
        project, blocks, [VMEM] * 2, [spread], 2 * devices * w_out.size, 2 * w_out.size, 4 * MIB
    )(*on_chip(columns.reshape(devices, features // devices), w_out_held))
    hid, copies = call(
        middle, (row, blocks), [VMEM] * 3, [], devices * width, 4 * devices * width, 2 * MIB
    )(*on_chip(exchange(parts), resid_rows, moe_rows))
    weight = pltpu.VMEM((hidden, width), bf16)
    outcome = call(
        experts,
        blocks,
        [VMEM] * 3 + [HBM] * 2,
        [
            spread,
            pltpu.VMEM((devices, width), bf16),
            weight,
            weight,
            pltpu.SemaphoreType.DMA((2 * WEIGHT_BLOCKS,)),
        ],
        6 * devices * hidden * width,
        6 * hidden * width,
        16 * MIB,
    )(*on_chip(exchange(copies), coef, w_gate_held), *off_chip(w_up, w_down))
    return call(
        finish,
        jax.ShapeDtypeStruct((1, width), bf16),
        [VMEM, VMEM],
        [],
        devices * width,
        2 * devices * width,
        2 * MIB,
    )(*on_chip(exchange(outcome), hid))


def solution(mesh):
    return jax.shard_map(
        shards,
        mesh=mesh,
        in_specs=(
            P(("group", "wide"), None),
            P(("group", "wide"), None),
            P(("group", "wide"), None),
            P(("group", "wide"), None),
            P(("group", "wide"), None, None, None),
            P(),
            P(("group", "wide"), None),
            P(),
            P("wide", None),
            P(),
            P("wide", None, None),
            P("wide", None, None),
            P("wide", None, None),
            P("group", None),
            P("group", None),
        ),
        out_specs=P(("group", "wide"), None),
        check_vma=False,
    )
```

```python
import jax
import jax.numpy as jnp
from jax import lax
from jax.experimental import pallas as pl
from jax.experimental.pallas import tpu as pltpu
from jax.sharding import PartitionSpec as P

SPLIT = 8
LANES = 128
HEAD_BLOCKS = 4
VMEM = pl.BlockSpec(memory_space=pltpu.VMEM)
HBM = pl.BlockSpec(memory_space=pltpu.HBM)
MIB = 1024 * 1024


def off_chip(*values):
    return [pltpu.with_memory_space_constraint(value, pltpu.HBM) for value in values]


def on_chip(*values):
    return [pltpu.with_memory_space_constraint(value, pltpu.VMEM) for value in values]


def call(body, out_shape, in_specs, scratch, flops, moved, limit):
    return pl.pallas_call(
        body,
        out_shape=out_shape,
        in_specs=in_specs,
        out_specs=jax.tree.map(lambda _: VMEM, out_shape),
        scratch_shapes=scratch,
        compiler_params=pltpu.CompilerParams(vmem_limit_bytes=limit),
        cost_estimate=pl.CostEstimate(flops=flops, bytes_accessed=moved, transcendentals=0),
    )


def exchange(blocks):
    return lax.all_to_all(blocks, "wide", split_axis=0, concat_axis=0, tiled=True)


def own_half(ref):
    half = ref.shape[1] // 2
    return pl.ds(pl.multiple_of(lax.rem(lax.axis_index("wide"), 2) * half, half), half)


def other_half(ref):
    half = ref.shape[1] // 2
    return pl.ds(pl.multiple_of((1 - lax.rem(lax.axis_index("wide"), 2)) * half, half), half)


def swap(value):
    devices = lax.axis_size("wide")
    return lax.ppermute(value, "wide", [(at, at ^ 1) for at in range(devices)])


def unfold(row_ref, held):
    for at in range(held.shape[0]):
        held[at : at + 1, :] = row_ref[0:1, at * LANES : (at + 1) * LANES].astype(jnp.float32)


def attention(
    query_ref, key_ref, value_ref, gate_ref, norm_ref, decay_ref, state_ref, resid_ref,
    moe_ref, ids_ref, weights_ref, w_out_ref,
    out_ref, resid_out, moe_out, coef_ref, w_out_half,
    rows, norm_held, decay_held, states, resid_held, ids_held, weights_held,
    q_held, k_held, v_held, g_held, att, sems,
):
    heads = decay_held.shape[0]
    block = heads // HEAD_BLOCKS
    started = []

    def fetch(source, target):
        copy = pltpu.make_async_copy(source, target, sems.at[len(started)])
        copy.start()
        started.append(copy)
        return copy

    small = [fetch(ref, rows.at[at]) for at, ref in enumerate((query_ref, key_ref))]
    small.append(fetch(decay_ref, decay_held))
    parts = [pl.ds(at * block, block) for at in range(HEAD_BLOCKS)]
    read = [fetch(state_ref.at[0, part], states.at[part]) for part in parts]
    later = [fetch(ref, rows.at[2 + at]) for at, ref in enumerate((value_ref, gate_ref))]
    later.append(fetch(norm_ref, norm_held))
    later.append(fetch(resid_ref, resid_held))
    later.append(fetch(ids_ref, ids_held))
    later.append(fetch(weights_ref, weights_held))
    last = [fetch(moe_ref, moe_out), fetch(w_out_ref.at[:, own_half(w_out_ref)], w_out_half)]

    for copy in small:
        copy.wait()
    unfold(rows.at[0], q_held)
    unfold(rows.at[1], k_held)
    q_rows = q_held[...]
    q_columns = q_rows.T
    both = jnp.sum(q_rows * k_held[...], axis=1, keepdims=True)
    for at in range(HEAD_BLOCKS):
        read[at].wait()
        for head in range(at * block, (at + 1) * block):
            seen = jnp.sum(q_columns[:, head : head + 1] * states[head], axis=0, keepdims=True)
            fade = jnp.exp(jnp.full((1, LANES), -decay_held[head], jnp.float32))
            att[head : head + 1, :] = fade * seen
    for copy in later:
        copy.wait()
    unfold(rows.at[2], v_held)
    unfold(rows.at[3], g_held)
    found = att[...] + both * v_held[...]
    scale = lax.rsqrt(jnp.sum(found * found, keepdims=True) / found.size + 1e-06)
    made = found * scale * norm_held[...] * jax.nn.sigmoid(g_held[...])
    if out_ref.shape[0] == heads:
        out_ref[...] = made
    else:
        att[...] = made
        for core in range(2):
            of_core = att[pl.ds(core, heads // 2, stride=2), :]
            out_ref[pl.ds(core, heads // 2, stride=4), :] = of_core
            out_ref[pl.ds(core + 2, heads // 2, stride=4), :] = of_core

    unfold(resid_held, resid_out)
    owner = lax.axis_index("wide") // SPLIT
    named = jnp.where(ids_held[...] == owner, weights_held[...], 0.0)
    along = jnp.sum(named, axis=0, keepdims=True)
    square = (coef_ref.shape[0], coef_ref.shape[0])
    same = lax.broadcasted_iota(jnp.int32, square, 0) == lax.broadcasted_iota(jnp.int32, square, 1)
    column = jnp.sum(jnp.where(same, along, 0.0), axis=1, keepdims=True)
    coef_ref[...] = jnp.broadcast_to(column, coef_ref.shape)
    for copy in last:
        copy.wait()


def columns_to_blocks(made, spread, out_ref):
    rows, groups, size, _ = out_ref.shape
    tiles = groups * size
    for tile in range(tiles):
        spread[pl.ds(tile, rows, stride=tiles), :] = made[:, tile * LANES : (tile + 1) * LANES]
    for row in range(rows):
        for group in range(groups):
            lines = spread[pl.ds(row * tiles + group * size, size), :]
            out_ref[row, group] = lines.astype(out_ref.dtype)


def blocks_to_columns(blocks_ref, spread, inputs):
    rows, groups, size, _ = blocks_ref.shape
    tiles = groups * size
    for row in range(rows):
        for group in range(groups):
            lines = pl.ds(row * tiles + group * size, size)
            spread[lines, :] = blocks_ref[row, group].astype(jnp.float32)
    for tile in range(tiles):
        inputs[:, tile * LANES : (tile + 1) * LANES] = spread[
            pl.ds(tile, rows, stride=tiles), :
        ].astype(jnp.bfloat16)
    return inputs[...]


def multiply(left, right):
    return jnp.dot(left, right, preferred_element_type=jnp.float32)


def by_rows(left, weight):
    return lax.dot_general(
        left, weight, (((1,), (1,)), ((), ())), preferred_element_type=jnp.float32
    )


def project(*refs):
    *column_refs, w_ref, w_other_ref, out_ref, spread = refs
    rows = out_ref.shape[0]
    if len(column_refs) == 1:
        pair = [column_refs[0][pl.ds(core, rows, stride=2), :] for core in range(2)]
    else:
        pair = [ref[...] for ref in column_refs]
    first = lax.rem(lax.axis_index("wide"), 2) == 0
    own = jnp.where(first, pair[0], pair[1]).astype(jnp.bfloat16)
    other = jnp.where(first, pair[1], pair[0]).astype(jnp.bfloat16)
    made = multiply(own, w_ref[...]) + multiply(other, w_other_ref[:, own_half(w_other_ref)])
    columns_to_blocks(made, spread, out_ref)


def add_up(parts_ref, held):
    devices, groups, size, _ = parts_ref.shape
    for half in range(2):
        total = parts_ref[half].astype(jnp.float32)
        for at in range(half + 2, devices, 2):
            total = total + parts_ref[at].astype(jnp.float32)
        for group in range(groups):
            start = (half * groups + group) * size
            held[start : start + size, :] = total[group]


def middle(parts_ref, resid_ref, gain_ref, hid_ref, copies_ref, held):
    devices, groups, size, _ = copies_ref.shape
    add_up(parts_ref, held)
    hid = (resid_ref[...] + held[...]).astype(jnp.bfloat16).astype(jnp.float32)
    hid_ref[...] = hid
    scale = lax.rsqrt(jnp.sum(hid * hid, keepdims=True) / hid.size + 1e-06)
    held[...] = hid * scale * gain_ref[...]
    for half in range(2):
        for group in range(groups):
            start = (half * groups + group) * size
            lines = held[start : start + size, :].astype(jnp.bfloat16)
            for at in range(half, devices, 2):
                copies_ref[at, group] = lines


def experts_own(blocks_ref, gate_ref, up_ref, gate_out, up_out, up_own, up_other, spread, inputs, sems):
    half = up_own.shape[1]
    copies = []
    for columns, target in ((own_half(gate_ref), up_own), (other_half(gate_ref), up_other)):
        copy = pltpu.make_async_copy(up_ref.at[0, :, columns], target, sems.at[len(copies)])
        copy.start()
        copies.append(copy)
    given = blocks_to_columns(blocks_ref, spread, inputs)
    gate_out[...] = by_rows(given, gate_ref[:, own_half(gate_ref)])
    copies[0].wait()
    up_out[...] = by_rows(given, up_own[...])
    copies[1].wait()


def experts_other(
    blocks_ref, gate_ref, up_other, gate_held, up_held, coef_ref, down_ref,
    inner_ref, send_ref, down_own, down_other, spread, inputs, sems,
):
    copies = []
    for columns, target in ((other_half(gate_ref), down_other), (own_half(gate_ref), down_own)):
        copy = pltpu.make_async_copy(down_ref.at[0, :, columns], target, sems.at[len(copies)])
        copy.start()
        copies.append(copy)
    given = blocks_to_columns(blocks_ref, spread, inputs)
    gate = gate_held[...] + by_rows(given, gate_ref[:, other_half(gate_ref)])
    upper = up_held[...] + by_rows(given, up_other[...])
    inner = (jax.nn.silu(gate) * upper).astype(jnp.bfloat16)
    inner_ref[...] = inner
    copies[0].wait()
    made = multiply(inner, down_other[...])
    coef = coef_ref[...]
    for at in range(0, made.shape[1], LANES):
        send_ref[:, at : at + LANES] = (made[:, at : at + LANES] * coef).astype(send_ref.dtype)
    copies[1].wait()


def experts_last(inner_ref, coef_ref, down_own, out_ref):
    made = multiply(inner_ref[...], down_own[...])
    coef = coef_ref[...]
    for at in range(0, made.shape[1], LANES):
        out_ref[:, at : at + LANES] = made[:, at : at + LANES] * coef


def join(own_ref, other_ref, out_ref, spread):
    columns_to_blocks(own_ref[...] + other_ref[...].astype(jnp.float32), spread, out_ref)


def finish(parts_ref, hid_ref, out_ref, held):
    add_up(parts_ref, held)
    held[...] = hid_ref[...] + held[...]
    for at in range(held.shape[0]):
        out_ref[0:1, at * LANES : (at + 1) * LANES] = held[at : at + 1, :].astype(out_ref.dtype)


def shards(
    resid,
    query,
    key,
    value,
    state,
    decay,
    out_gate,
    norm_gain,
    w_out,
    moe_gain,
    w_gate,
    w_up,
    w_down,
    expert_ids,
    expert_weights,
):
    width = resid.shape[1]
    half = width // 2
    heads = decay.shape[0]
    features = query.shape[1]
    devices = lax.axis_size("wide")
    each = features // devices
    tiles = width // LANES
    hidden = w_gate.shape[1]
    size = next(size for size in (8, 4, 2, 1) if tiles // 2 % size == 0)
    f32, bf16 = jnp.float32, jnp.bfloat16
    row = pltpu.VMEM((tiles, LANES), f32)
    blocks = pltpu.VMEM((devices, tiles // 2 // size, size, LANES), bf16)
    spread = pltpu.VMEM((devices * tiles // 2, LANES), f32)
    per_head = pltpu.VMEM((heads, LANES), f32)
    paired = each == LANES

    attn, resid_rows, moe_rows, coef, w_out_half = call(
        attention,
        (
            pltpu.VMEM((2 * heads if paired else heads, LANES), f32),
            row,
            row,
            pltpu.VMEM((devices, LANES), f32),
            pltpu.VMEM((each, half), bf16),
        ),
        [HBM] * 12,
        [
            pltpu.VMEM((4, 1, features), bf16),
            per_head,
            pltpu.SMEM((heads,), f32),
            pltpu.VMEM(state.shape[1:], f32),
            pltpu.VMEM((1, width), bf16),
            pltpu.VMEM((2, devices), jnp.int32),
            pltpu.VMEM((2, devices), f32),
        ]
        + [per_head] * 5
        + [pltpu.SemaphoreType.DMA((11 + HEAD_BLOCKS,))],
        2 * state.size,
        4 * state.size,
        8 * MIB,
    )(
        *off_chip(
            query,
            key,
            value,
            out_gate,
            norm_gain.reshape(heads, LANES),
            decay,
            state,
            resid,
            moe_gain.reshape(tiles, LANES),
            expert_ids.T,
            expert_weights.T,
            w_out,
        )
    )
    w_out_other = swap(w_out)
    if paired:
        columns = exchange(attn.reshape(devices, 2, LANES))
        columns = [columns.reshape(2 * devices, LANES)]
    else:
        attn = jnp.repeat(attn.reshape(devices // 2, 2, each), 2, axis=0)
        columns = exchange(attn)
        columns = [columns[:, core] for core in range(2)]
    parts = call(
        project,
        blocks,
        [VMEM] * (2 + len(columns)),
        [spread],
        2 * devices * w_out.size,
        2 * w_out.size,
        4 * MIB,
    )(*on_chip(*columns, w_out_half, w_out_other))
    hid, copies = call(
        middle, (row, blocks), [VMEM] * 3, [row], devices * width, 4 * devices * width, 2 * MIB
    )(*on_chip(exchange(parts), resid_rows, moe_rows))
    given = exchange(copies)
    given_other = swap(given)
    inputs = pltpu.VMEM((devices, half), bf16)
    partial_sum = pltpu.VMEM((devices, hidden), f32)
    weight = pltpu.VMEM((hidden, half), bf16)
    gate_weight = w_gate.reshape(w_gate.shape[1:])
    *sums, up_other = call(
        lambda blocks_ref, gate_ref, up_ref, gate_out, up_out, up_other, *rest: experts_own(
            blocks_ref, gate_ref, up_ref, gate_out, up_out, rest[0], up_other, *rest[1:]
        ),
        (partial_sum, partial_sum, weight),
        [VMEM] * 2 + [HBM],
        [weight, spread, inputs, pltpu.SemaphoreType.DMA((2,))],
        2 * devices * hidden * width,
        4 * hidden * width,
        8 * MIB,
    )(*on_chip(given, gate_weight), *off_chip(w_up))
    inner, send, down_own = call(
        experts_other,
        (pltpu.VMEM((devices, hidden), bf16), inputs, weight),
        [VMEM] * 6 + [HBM],
        [weight, spread, inputs, pltpu.SemaphoreType.DMA((2,))],
        3 * devices * hidden * width,
        4 * hidden * width,
        8 * MIB,
    )(*on_chip(given_other, gate_weight, up_other, *sums, coef), *off_chip(w_down))
    received = swap(send)
    own = call(
        experts_last,
        pltpu.VMEM((devices, half), f32),
        [VMEM] * 3,
        [],
        devices * hidden * width,
        hidden * width,
        4 * MIB,
    )(*on_chip(inner, coef, down_own))
    outcome = call(
        join, blocks, [VMEM] * 2, [spread], devices * width, 4 * devices * width, 4 * MIB
    )(*on_chip(own, received))
    return call(
        finish,
        jax.ShapeDtypeStruct((1, width), bf16),
        [VMEM, VMEM],
        [row],
        devices * width,
        2 * devices * width,
        2 * MIB,
    )(*on_chip(exchange(outcome), hid))


def solution(mesh):
    return jax.shard_map(
        shards,
        mesh=mesh,
        in_specs=(
            P(("group", "wide"), None),
            P(("group", "wide"), None),
            P(("group", "wide"), None),
            P(("group", "wide"), None),
            P(("group", "wide"), None, None, None),
            P(),
            P(("group", "wide"), None),
            P(),
            P("wide", None),
            P(),
            P("wide", None, None),
            P("wide", None, None),
            P("wide", None, None),
            P("group", None),
            P("group", None),
        ),
        out_specs=P(("group", "wide"), None),
        check_vma=False,
    )
```

```python
import jax
import jax.numpy as jnp
from jax import lax
from jax.experimental import pallas as pl
from jax.experimental.pallas import tpu as pltpu
from jax.sharding import PartitionSpec as P

SPLIT = 8
LANES = 128
HEAD_BLOCKS = 4
VMEM = pl.BlockSpec(memory_space=pltpu.VMEM)
HBM = pl.BlockSpec(memory_space=pltpu.HBM)
MIB = 1024 * 1024


def off_chip(*values):
    return [pltpu.with_memory_space_constraint(value, pltpu.HBM) for value in values]


def on_chip(*values):
    return [pltpu.with_memory_space_constraint(value, pltpu.VMEM) for value in values]


def call(body, out_shape, in_specs, scratch, flops, moved, limit):
    return pl.pallas_call(
        body,
        out_shape=out_shape,
        in_specs=in_specs,
        out_specs=jax.tree.map(lambda _: VMEM, out_shape),
        scratch_shapes=scratch,
        compiler_params=pltpu.CompilerParams(vmem_limit_bytes=limit),
        cost_estimate=pl.CostEstimate(flops=flops, bytes_accessed=moved, transcendentals=0),
    )


def exchange(blocks):
    return lax.all_to_all(blocks, "wide", split_axis=0, concat_axis=0, tiled=True)


def own_half(ref):
    half = ref.shape[1] // 2
    return pl.ds(pl.multiple_of(lax.rem(lax.axis_index("wide"), 2) * half, half), half)


def other_half(ref):
    half = ref.shape[1] // 2
    return pl.ds(pl.multiple_of((1 - lax.rem(lax.axis_index("wide"), 2)) * half, half), half)


def swap(value):
    devices = lax.axis_size("wide")
    return lax.ppermute(value, "wide", [(at, at ^ 1) for at in range(devices)])


def unfold(row_ref, held):
    for at in range(held.shape[0]):
        held[at : at + 1, :] = row_ref[0:1, at * LANES : (at + 1) * LANES].astype(jnp.float32)


def attention(
    query_ref, key_ref, value_ref, gate_ref, norm_ref, decay_ref, state_ref, resid_ref,
    moe_ref, ids_ref, weights_ref, w_out_ref,
    out_ref, resid_out, moe_out, coef_ref, w_out_half,
    rows, norm_held, decay_held, states, resid_held, ids_held, weights_held,
    q_held, k_held, v_held, g_held, att, sems,
):
    heads = decay_held.shape[0]
    block = heads // HEAD_BLOCKS
    started = []

    def fetch(source, target):
        copy = pltpu.make_async_copy(source, target, sems.at[len(started)])
        copy.start()
        started.append(copy)
        return copy

    small = [fetch(ref, rows.at[at]) for at, ref in enumerate((query_ref, key_ref))]
    small.append(fetch(decay_ref, decay_held))
    parts = [pl.ds(at * block, block) for at in range(HEAD_BLOCKS)]
    read = [fetch(state_ref.at[0, part], states.at[part]) for part in parts]
    later = [fetch(ref, rows.at[2 + at]) for at, ref in enumerate((value_ref, gate_ref))]
    later.append(fetch(norm_ref, norm_held))
    later.append(fetch(resid_ref, resid_held))
    later.append(fetch(ids_ref, ids_held))
    later.append(fetch(weights_ref, weights_held))
    last = [fetch(moe_ref, moe_out), fetch(w_out_ref.at[:, own_half(w_out_ref)], w_out_half)]

    for copy in small:
        copy.wait()
    unfold(rows.at[0], q_held)
    unfold(rows.at[1], k_held)
    q_rows = q_held[...]
    q_columns = q_rows.T
    both = jnp.sum(q_rows * k_held[...], axis=1, keepdims=True)
    for at in range(HEAD_BLOCKS):
        read[at].wait()
        for head in range(at * block, (at + 1) * block):
            seen = jnp.sum(q_columns[:, head : head + 1] * states[head], axis=0, keepdims=True)
            fade = jnp.exp(jnp.full((1, LANES), -decay_held[head], jnp.float32))
            att[head : head + 1, :] = fade * seen
    for copy in later:
        copy.wait()
    unfold(rows.at[2], v_held)
    unfold(rows.at[3], g_held)
    found = att[...] + both * v_held[...]
    scale = lax.rsqrt(jnp.sum(found * found, keepdims=True) / found.size + 1e-06)
    made = found * scale * norm_held[...] * jax.nn.sigmoid(g_held[...])
    if out_ref.shape[0] == heads:
        out_ref[...] = made
    else:
        att[...] = made
        for core in range(2):
            of_core = att[pl.ds(core, heads // 2, stride=2), :]
            out_ref[pl.ds(core, heads // 2, stride=4), :] = of_core
            out_ref[pl.ds(core + 2, heads // 2, stride=4), :] = of_core

    unfold(resid_held, resid_out)
    owner = lax.axis_index("wide") // SPLIT
    named = jnp.where(ids_held[...] == owner, weights_held[...], 0.0)
    along = jnp.sum(named, axis=0, keepdims=True)
    square = (coef_ref.shape[0], coef_ref.shape[0])
    same = lax.broadcasted_iota(jnp.int32, square, 0) == lax.broadcasted_iota(jnp.int32, square, 1)
    column = jnp.sum(jnp.where(same, along, 0.0), axis=1, keepdims=True)
    coef_ref[...] = jnp.broadcast_to(column, coef_ref.shape)
    for copy in last:
        copy.wait()


def columns_to_blocks(made, spread, out_ref):
    rows, groups, size, _ = out_ref.shape
    tiles = groups * size
    for tile in range(tiles):
        spread[pl.ds(tile, rows, stride=tiles), :] = made[:, tile * LANES : (tile + 1) * LANES]
    for row in range(rows):
        for group in range(groups):
            lines = spread[pl.ds(row * tiles + group * size, size), :]
            out_ref[row, group] = lines.astype(out_ref.dtype)


def blocks_to_columns(blocks_ref, spread, inputs):
    rows, groups, size, _ = blocks_ref.shape
    tiles = groups * size
    for row in range(rows):
        for group in range(groups):
            lines = pl.ds(row * tiles + group * size, size)
            spread[lines, :] = blocks_ref[row, group].astype(jnp.float32)
    for tile in range(tiles):
        inputs[:, tile * LANES : (tile + 1) * LANES] = spread[
            pl.ds(tile, rows, stride=tiles), :
        ].astype(jnp.bfloat16)
    return inputs[...]


def multiply(left, right):
    return jnp.dot(left, right, preferred_element_type=jnp.float32)


def by_rows(left, weight):
    return lax.dot_general(
        left, weight, (((1,), (1,)), ((), ())), preferred_element_type=jnp.float32
    )


def project(*refs):
    *column_refs, w_ref, w_other_ref, _up_ref, _down_ref, out_ref, spread = refs
    rows = out_ref.shape[0]
    if len(column_refs) == 1:
        pair = [column_refs[0][pl.ds(core, rows, stride=2), :] for core in range(2)]
    else:
        pair = [ref[...] for ref in column_refs]
    first = lax.rem(lax.axis_index("wide"), 2) == 0
    own = jnp.where(first, pair[0], pair[1]).astype(jnp.bfloat16)
    other = jnp.where(first, pair[1], pair[0]).astype(jnp.bfloat16)
    made = multiply(own, w_ref[...]) + multiply(other, w_other_ref[:, own_half(w_other_ref)])
    columns_to_blocks(made, spread, out_ref)


def add_up(parts_ref, held):
    devices, groups, size, _ = parts_ref.shape
    for half in range(2):
        total = parts_ref[half].astype(jnp.float32)
        for at in range(half + 2, devices, 2):
            total = total + parts_ref[at].astype(jnp.float32)
        for group in range(groups):
            start = (half * groups + group) * size
            held[start : start + size, :] = total[group]


def middle(parts_ref, resid_ref, gain_ref, _up_ref, _down_ref, hid_ref, copies_ref, held):
    devices, groups, size, _ = copies_ref.shape
    add_up(parts_ref, held)
    hid = (resid_ref[...] + held[...]).astype(jnp.bfloat16).astype(jnp.float32)
    hid_ref[...] = hid
    scale = lax.rsqrt(jnp.sum(hid * hid, keepdims=True) / hid.size + 1e-06)
    held[...] = hid * scale * gain_ref[...]
    for half in range(2):
        for group in range(groups):
            start = (half * groups + group) * size
            lines = held[start : start + size, :].astype(jnp.bfloat16)
            for at in range(half, devices, 2):
                copies_ref[at, group] = lines


def experts_own(blocks_ref, gate_ref, up_ref, gate_out, up_out, spread, inputs):
    given = blocks_to_columns(blocks_ref, spread, inputs)
    gate_out[...] = by_rows(given, gate_ref[:, own_half(gate_ref)])
    up_out[...] = by_rows(given, up_ref[:, own_half(up_ref)])


def experts_other(
    blocks_ref, gate_ref, up_ref, down_ref, gate_held, up_held, coef_ref,
    inner_ref, send_ref, spread, inputs,
):
    given = blocks_to_columns(blocks_ref, spread, inputs)
    gate = gate_held[...] + by_rows(given, gate_ref[:, other_half(gate_ref)])
    upper = up_held[...] + by_rows(given, up_ref[:, other_half(up_ref)])
    inner = (jax.nn.silu(gate) * upper).astype(jnp.bfloat16)
    inner_ref[...] = inner
    made = multiply(inner, down_ref[:, other_half(down_ref)])
    coef = coef_ref[...]
    for at in range(0, made.shape[1], LANES):
        send_ref[:, at : at + LANES] = (made[:, at : at + LANES] * coef).astype(send_ref.dtype)


def experts_last(inner_ref, coef_ref, down_ref, out_ref):
    made = multiply(inner_ref[...], down_ref[:, own_half(down_ref)])
    coef = coef_ref[...]
    for at in range(0, made.shape[1], LANES):
        out_ref[:, at : at + LANES] = made[:, at : at + LANES] * coef


def join(own_ref, other_ref, out_ref, spread):
    columns_to_blocks(own_ref[...] + other_ref[...].astype(jnp.float32), spread, out_ref)


def finish(parts_ref, hid_ref, out_ref, held):
    add_up(parts_ref, held)
    held[...] = hid_ref[...] + held[...]
    for at in range(held.shape[0]):
        out_ref[0:1, at * LANES : (at + 1) * LANES] = held[at : at + 1, :].astype(out_ref.dtype)


def shards(
    resid,
    query,
    key,
    value,
    state,
    decay,
    out_gate,
    norm_gain,
    w_out,
    moe_gain,
    w_gate,
    w_up,
    w_down,
    expert_ids,
    expert_weights,
):
    width = resid.shape[1]
    half = width // 2
    heads = decay.shape[0]
    features = query.shape[1]
    devices = lax.axis_size("wide")
    each = features // devices
    tiles = width // LANES
    hidden = w_gate.shape[1]
    size = next(size for size in (8, 4, 2, 1) if tiles // 2 % size == 0)
    f32, bf16 = jnp.float32, jnp.bfloat16
    row = pltpu.VMEM((tiles, LANES), f32)
    blocks = pltpu.VMEM((devices, tiles // 2 // size, size, LANES), bf16)
    spread = pltpu.VMEM((devices * tiles // 2, LANES), f32)
    per_head = pltpu.VMEM((heads, LANES), f32)
    paired = each == LANES

    attn, resid_rows, moe_rows, coef, w_out_half = call(
        attention,
        (
            pltpu.VMEM((2 * heads if paired else heads, LANES), f32),
            row,
            row,
            pltpu.VMEM((devices, LANES), f32),
            pltpu.VMEM((each, half), bf16),
        ),
        [HBM] * 12,
        [
            pltpu.VMEM((4, 1, features), bf16),
            per_head,
            pltpu.SMEM((heads,), f32),
            pltpu.VMEM(state.shape[1:], f32),
            pltpu.VMEM((1, width), bf16),
            pltpu.VMEM((2, devices), jnp.int32),
            pltpu.VMEM((2, devices), f32),
        ]
        + [per_head] * 5
        + [pltpu.SemaphoreType.DMA((11 + HEAD_BLOCKS,))],
        2 * state.size,
        4 * state.size,
        8 * MIB,
    )(
        *off_chip(
            query,
            key,
            value,
            out_gate,
            norm_gain.reshape(heads, LANES),
            decay,
            state,
            resid,
            moe_gain.reshape(tiles, LANES),
            expert_ids.T,
            expert_weights.T,
            w_out,
        )
    )
    w_out_other = swap(w_out)
    w_gate, w_up, w_down = (w.reshape(w.shape[1:]) for w in (w_gate, w_up, w_down))
    if paired:
        columns = exchange(attn.reshape(devices, 2, LANES))
        columns = [columns.reshape(2 * devices, LANES)]
    else:
        attn = jnp.repeat(attn.reshape(devices // 2, 2, each), 2, axis=0)
        columns = exchange(attn)
        columns = [columns[:, core] for core in range(2)]
    parts = call(
        project,
        blocks,
        [VMEM] * (2 + len(columns)) + [HBM] * 2,
        [spread],
        2 * devices * w_out.size,
        2 * w_out.size,
        4 * MIB,
    )(*on_chip(*columns, w_out_half, w_out_other), *off_chip(w_up, w_down))
    hid, copies = call(
        middle, (row, blocks), [VMEM] * 5, [row], devices * width, 4 * devices * width, 2 * MIB
    )(*on_chip(exchange(parts), resid_rows, moe_rows, w_up, w_down))
    given = exchange(copies)
    given_other = swap(given)
    inputs = pltpu.VMEM((devices, half), bf16)
    partial_sum = pltpu.VMEM((devices, hidden), f32)
    sums = call(
        experts_own,
        (partial_sum, partial_sum),
        [VMEM] * 3,
        [spread, inputs],
        2 * devices * hidden * width,
        4 * hidden * width,
        8 * MIB,
    )(*on_chip(given, w_gate, w_up))
    inner, send = call(
        experts_other,
        (pltpu.VMEM((devices, hidden), bf16), inputs),
        [VMEM] * 7,
        [spread, inputs],
        3 * devices * hidden * width,
        4 * hidden * width,
        8 * MIB,
    )(*on_chip(given_other, w_gate, w_up, w_down, *sums, coef))
    received = swap(send)
    own = call(
        experts_last,
        pltpu.VMEM((devices, half), f32),
        [VMEM] * 3,
        [],
        devices * hidden * width,
        hidden * width,
        4 * MIB,
    )(*on_chip(inner, coef, w_down))
    outcome = call(
        join, blocks, [VMEM] * 2, [spread], devices * width, 4 * devices * width, 4 * MIB
    )(*on_chip(own, received))
    return call(
        finish,
        jax.ShapeDtypeStruct((1, width), bf16),
        [VMEM, VMEM],
        [row],
        devices * width,
        2 * devices * width,
        2 * MIB,
    )(*on_chip(exchange(outcome), hid))


def solution(mesh):
    return jax.shard_map(
        shards,
        mesh=mesh,
        in_specs=(
            P(("group", "wide"), None),
            P(("group", "wide"), None),
            P(("group", "wide"), None),
            P(("group", "wide"), None),
            P(("group", "wide"), None, None, None),
            P(),
            P(("group", "wide"), None),
            P(),
            P("wide", None),
            P(),
            P("wide", None, None),
            P("wide", None, None),
            P("wide", None, None),
            P("group", None),
            P("group", None),
        ),
        out_specs=P(("group", "wide"), None),
        check_vma=False,
    )
```

```python
import jax
import jax.numpy as jnp
from jax import lax
from jax.experimental import pallas as pl
from jax.experimental.pallas import tpu as pltpu
from jax.sharding import PartitionSpec as P

SPLIT = 8
LANES = 128
HEAD_BLOCKS = 4
VMEM = pl.BlockSpec(memory_space=pltpu.VMEM)
HBM = pl.BlockSpec(memory_space=pltpu.HBM)
MIB = 1024 * 1024


def off_chip(*values):
    return [pltpu.with_memory_space_constraint(value, pltpu.HBM) for value in values]


def on_chip(*values):
    return [pltpu.with_memory_space_constraint(value, pltpu.VMEM) for value in values]


def call(body, out_shape, in_specs, scratch, flops, moved, limit):
    return pl.pallas_call(
        body,
        out_shape=out_shape,
        in_specs=in_specs,
        out_specs=jax.tree.map(lambda _: VMEM, out_shape),
        scratch_shapes=scratch,
        compiler_params=pltpu.CompilerParams(vmem_limit_bytes=limit),
        cost_estimate=pl.CostEstimate(flops=flops, bytes_accessed=moved, transcendentals=0),
    )


def exchange(blocks):
    return lax.all_to_all(blocks, "wide", split_axis=0, concat_axis=0, tiled=True)


def own_half(ref):
    half = ref.shape[1] // 2
    return pl.ds(pl.multiple_of(lax.rem(lax.axis_index("wide"), 2) * half, half), half)


def other_half(ref):
    half = ref.shape[1] // 2
    return pl.ds(pl.multiple_of((1 - lax.rem(lax.axis_index("wide"), 2)) * half, half), half)


def swap(value):
    devices = lax.axis_size("wide")
    return lax.ppermute(value, "wide", [(at, at ^ 1) for at in range(devices)])


def unfold(row_ref, held):
    held[...] = row_ref[...].astype(jnp.float32).reshape(held.shape)


def attention(
    query_ref, key_ref, value_ref, gate_ref, norm_ref, decay_ref, state_ref,
    ids_ref, weights_ref, w_out_ref, out_ref, coef_ref, w_out_half,
    rows, norm_held, decay_held, states, ids_held, weights_held,
    q_held, k_held, v_held, g_held, att, q_wide, sems,
):
    heads = decay_held.shape[0]
    block = heads // HEAD_BLOCKS
    started = []

    def fetch(source, target):
        copy = pltpu.make_async_copy(source, target, sems.at[len(started)])
        copy.start()
        started.append(copy)
        return copy

    small = [fetch(ref, rows.at[at]) for at, ref in enumerate((query_ref, key_ref))]
    small.append(fetch(decay_ref, decay_held))
    parts = [pl.ds(at * block, block) for at in range(HEAD_BLOCKS)]
    read = [fetch(state_ref.at[0, part], states.at[part]) for part in parts]
    later = [fetch(ref, rows.at[2 + at]) for at, ref in enumerate((value_ref, gate_ref))]
    later.append(fetch(norm_ref, norm_held))
    later.append(fetch(ids_ref, ids_held))
    later.append(fetch(weights_ref, weights_held))
    last = [fetch(w_out_ref.at[:, own_half(w_out_ref)], w_out_half)]

    for copy in small:
        copy.wait()
    unfold(rows.at[0], q_held)
    unfold(rows.at[1], k_held)
    q_rows = q_held[...]
    q_columns = q_rows.T
    both = jnp.sum(q_rows * k_held[...], axis=1, keepdims=True)
    for head in range(heads):
        q_wide[head] = jnp.broadcast_to(q_columns[:, head : head + 1], q_wide.shape[1:])
    for at in range(HEAD_BLOCKS):
        read[at].wait()
        for head in range(at * block, (at + 1) * block):
            seen = jnp.sum(q_wide[head] * states[head], axis=0, keepdims=True)
            fade = jnp.exp(jnp.full((1, LANES), -decay_held[head], jnp.float32))
            att[head : head + 1, :] = fade * seen
    for copy in later:
        copy.wait()
    unfold(rows.at[2], v_held)
    unfold(rows.at[3], g_held)
    found = att[...] + both * v_held[...]
    scale = lax.rsqrt(jnp.sum(found * found, keepdims=True) / found.size + 1e-06)
    made = found * scale * norm_held[...] * jax.nn.sigmoid(g_held[...])
    if out_ref.shape[0] == heads:
        out_ref[...] = made
    else:
        att[...] = made
        for core in range(2):
            of_core = att[pl.ds(core, heads // 2, stride=2), :]
            out_ref[pl.ds(core, heads // 2, stride=4), :] = of_core
            out_ref[pl.ds(core + 2, heads // 2, stride=4), :] = of_core

    owner = lax.axis_index("wide") // SPLIT
    named = jnp.where(ids_held[...] == owner, weights_held[...], 0.0)
    along = jnp.sum(named, axis=0, keepdims=True)
    square = (coef_ref.shape[0], coef_ref.shape[0])
    same = lax.broadcasted_iota(jnp.int32, square, 0) == lax.broadcasted_iota(jnp.int32, square, 1)
    column = jnp.sum(jnp.where(same, along, 0.0), axis=1, keepdims=True)
    coef_ref[...] = jnp.broadcast_to(column, coef_ref.shape)
    for copy in last:
        copy.wait()


def columns_to_blocks(made, spread, out_ref):
    rows, groups, size, _ = out_ref.shape
    tiles = groups * size
    for tile in range(tiles):
        spread[pl.ds(tile, rows, stride=tiles), :] = made[:, tile * LANES : (tile + 1) * LANES]
    for row in range(rows):
        for group in range(groups):
            lines = spread[pl.ds(row * tiles + group * size, size), :]
            out_ref[row, group] = lines.astype(out_ref.dtype)


def blocks_to_columns(blocks_ref, spread, inputs):
    rows, groups, size, _ = blocks_ref.shape
    tiles = groups * size
    for row in range(rows):
        for group in range(groups):
            lines = pl.ds(row * tiles + group * size, size)
            spread[lines, :] = blocks_ref[row, group].astype(jnp.float32)
    for tile in range(tiles):
        inputs[:, tile * LANES : (tile + 1) * LANES] = spread[
            pl.ds(tile, rows, stride=tiles), :
        ].astype(jnp.bfloat16)
    return inputs[...]


def multiply(left, right):
    return jnp.dot(left, right, preferred_element_type=jnp.float32)


def by_rows(left, weight):
    return lax.dot_general(
        left, weight, (((1,), (1,)), ((), ())), preferred_element_type=jnp.float32
    )


def project(*refs):
    *column_refs, w_ref, w_other_ref, _up_ref, _down_ref, _gate_ref, out_ref, spread = refs
    rows = out_ref.shape[0]
    if len(column_refs) == 1:
        pair = [column_refs[0][pl.ds(core, rows, stride=2), :] for core in range(2)]
    else:
        pair = [ref[...] for ref in column_refs]
    first = lax.rem(lax.axis_index("wide"), 2) == 0
    own = jnp.where(first, pair[0], pair[1]).astype(jnp.bfloat16)
    other = jnp.where(first, pair[1], pair[0]).astype(jnp.bfloat16)
    made = multiply(own, w_ref[...]) + multiply(other, w_other_ref[:, own_half(w_other_ref)])
    columns_to_blocks(made, spread, out_ref)


def add_up(parts_ref, held):
    devices, groups, size, _ = parts_ref.shape
    for half in range(2):
        total = parts_ref[half].astype(jnp.float32)
        for at in range(half + 2, devices, 2):
            total = total + parts_ref[at].astype(jnp.float32)
        for group in range(groups):
            start = (half * groups + group) * size
            held[start : start + size, :] = total[group]


def middle(parts_ref, resid_ref, gain_ref, _up_ref, _down_ref, _gate_ref, hid_ref, copies_ref, held, resid_rows):
    devices, groups, size, _ = copies_ref.shape
    add_up(parts_ref, held)
    unfold(resid_ref, resid_rows)
    hid = (resid_rows[...] + held[...]).astype(jnp.bfloat16).astype(jnp.float32)
    hid_ref[...] = hid
    scale = lax.rsqrt(jnp.sum(hid * hid, keepdims=True) / hid.size + 1e-06)
    held[...] = hid * scale * gain_ref[...]
    for half in range(2):
        for group in range(groups):
            start = (half * groups + group) * size
            lines = held[start : start + size, :].astype(jnp.bfloat16)
            for at in range(half, devices, 2):
                copies_ref[at, group] = lines


def experts_own(blocks_ref, gate_ref, up_ref, gate_out, up_out, spread, inputs):
    given = blocks_to_columns(blocks_ref, spread, inputs)
    gate_out[...] = by_rows(given, gate_ref[:, own_half(gate_ref)])
    up_out[...] = by_rows(given, up_ref[:, own_half(up_ref)])


def experts_other(
    blocks_ref, gate_ref, up_ref, down_ref, gate_held, up_held, coef_ref,
    inner_ref, send_ref, spread, inputs,
):
    given = blocks_to_columns(blocks_ref, spread, inputs)
    gate = gate_held[...] + by_rows(given, gate_ref[:, other_half(gate_ref)])
    upper = up_held[...] + by_rows(given, up_ref[:, other_half(up_ref)])
    inner = (jax.nn.silu(gate) * upper).astype(jnp.bfloat16)
    inner_ref[...] = inner
    made = multiply(inner, down_ref[:, other_half(down_ref)])
    coef = coef_ref[...]
    for at in range(0, made.shape[1], LANES):
        send_ref[:, at : at + LANES] = (made[:, at : at + LANES] * coef).astype(send_ref.dtype)


def experts_last(inner_ref, coef_ref, down_ref, out_ref):
    made = multiply(inner_ref[...], down_ref[:, own_half(down_ref)])
    coef = coef_ref[...]
    for at in range(0, made.shape[1], LANES):
        out_ref[:, at : at + LANES] = made[:, at : at + LANES] * coef


def join(own_ref, other_ref, out_ref, spread):
    columns_to_blocks(own_ref[...] + other_ref[...].astype(jnp.float32), spread, out_ref)


def finish(parts_ref, hid_ref, out_ref, held):
    add_up(parts_ref, held)
    held[...] = hid_ref[...] + held[...]
    for at in range(held.shape[0]):
        out_ref[0:1, at * LANES : (at + 1) * LANES] = held[at : at + 1, :].astype(out_ref.dtype)


def shards(
    resid,
    query,
    key,
    value,
    state,
    decay,
    out_gate,
    norm_gain,
    w_out,
    moe_gain,
    w_gate,
    w_up,
    w_down,
    expert_ids,
    expert_weights,
):
    width = resid.shape[1]
    half = width // 2
    heads = decay.shape[0]
    features = query.shape[1]
    devices = lax.axis_size("wide")
    each = features // devices
    tiles = width // LANES
    hidden = w_gate.shape[1]
    size = next(size for size in (8, 4, 2, 1) if tiles // 2 % size == 0)
    f32, bf16 = jnp.float32, jnp.bfloat16
    row = pltpu.VMEM((tiles, LANES), f32)
    blocks = pltpu.VMEM((devices, tiles // 2 // size, size, LANES), bf16)
    spread = pltpu.VMEM((devices * tiles // 2, LANES), f32)
    per_head = pltpu.VMEM((heads, LANES), f32)
    paired = each == LANES

    attn, coef, w_out_half = call(
        attention,
        (
            pltpu.VMEM((2 * heads if paired else heads, LANES), f32),
            pltpu.VMEM((devices, LANES), f32),
            pltpu.VMEM((each, half), bf16),
        ),
        [HBM] * 10,
        [
            pltpu.VMEM((4, 1, features), bf16),
            per_head,
            pltpu.SMEM((heads,), f32),
            pltpu.VMEM(state.shape[1:], f32),
            pltpu.VMEM((2, devices), jnp.int32),
            pltpu.VMEM((2, devices), f32),
        ]
        + [per_head] * 5
        + [pltpu.VMEM(state.shape[1:], f32)]
        + [pltpu.SemaphoreType.DMA((9 + HEAD_BLOCKS,))],
        2 * state.size,
        4 * state.size,
        8 * MIB,
    )(
        *off_chip(
            query,
            key,
            value,
            out_gate,
            norm_gain.reshape(heads, LANES),
            decay,
            state,
            expert_ids.T,
            expert_weights.T,
            w_out,
        )
    )
    w_out_other = swap(w_out)
    w_gate, w_up, w_down = (w.reshape(w.shape[1:]) for w in (w_gate, w_up, w_down))
    if paired:
        columns = exchange(attn.reshape(devices, 2, LANES))
        columns = [columns.reshape(2 * devices, LANES)]
    else:
        attn = jnp.repeat(attn.reshape(devices // 2, 2, each), 2, axis=0)
        columns = exchange(attn)
        columns = [columns[:, core] for core in range(2)]
    parts = call(
        project,
        blocks,
        [VMEM] * (2 + len(columns)) + [HBM] * 3,
        [spread],
        2 * devices * w_out.size,
        2 * w_out.size,
        4 * MIB,
    )(*on_chip(*columns, w_out_half, w_out_other), *off_chip(w_up, w_down, w_gate))
    hid, copies = call(
        middle, (row, blocks), [VMEM] * 6, [row, row], devices * width, 4 * devices * width, 2 * MIB
    )(*on_chip(exchange(parts), resid, moe_gain.reshape(tiles, LANES), w_up, w_down, w_gate))
    given = exchange(copies)
    given_other = swap(given)
    inputs = pltpu.VMEM((devices, half), bf16)
    partial_sum = pltpu.VMEM((devices, hidden), f32)
    sums = call(
        experts_own,
        (partial_sum, partial_sum),
        [VMEM] * 3,
        [spread, inputs],
        2 * devices * hidden * width,
        4 * hidden * width,
        8 * MIB,
    )(*on_chip(given, w_gate, w_up))
    inner, send = call(
        experts_other,
        (pltpu.VMEM((devices, hidden), bf16), inputs),
        [VMEM] * 7,
        [spread, inputs],
        3 * devices * hidden * width,
        4 * hidden * width,
        8 * MIB,
    )(*on_chip(given_other, w_gate, w_up, w_down, *sums, coef))
    received = swap(send)
    own = call(
        experts_last,
        pltpu.VMEM((devices, half), f32),
        [VMEM] * 3,
        [],
        devices * hidden * width,
        hidden * width,
        4 * MIB,
    )(*on_chip(inner, coef, w_down))
    outcome = call(
        join, blocks, [VMEM] * 2, [spread], devices * width, 4 * devices * width, 4 * MIB
    )(*on_chip(own, received))
    return call(
        finish,
        jax.ShapeDtypeStruct((1, width), bf16),
        [VMEM, VMEM],
        [row],
        devices * width,
        2 * devices * width,
        2 * MIB,
    )(*on_chip(exchange(outcome), hid))


def solution(mesh):
    return jax.shard_map(
        shards,
        mesh=mesh,
        in_specs=(
            P(("group", "wide"), None),
            P(("group", "wide"), None),
            P(("group", "wide"), None),
            P(("group", "wide"), None),
            P(("group", "wide"), None, None, None),
            P(),
            P(("group", "wide"), None),
            P(),
            P("wide", None),
            P(),
            P("wide", None, None),
            P("wide", None, None),
            P("wide", None, None),
            P("group", None),
            P("group", None),
        ),
        out_specs=P(("group", "wide"), None),
        check_vma=False,
    )
```

```python
import jax
import jax.numpy as jnp
from jax import lax
from jax.experimental import pallas as pl
from jax.experimental.pallas import tpu as pltpu
from jax.sharding import PartitionSpec as P

SPLIT = 8
LANES = 128
HEAD_BLOCKS = 4
VMEM = pl.BlockSpec(memory_space=pltpu.VMEM)
HBM = pl.BlockSpec(memory_space=pltpu.HBM)
MIB = 1024 * 1024


def off_chip(*values):
    return [pltpu.with_memory_space_constraint(value, pltpu.HBM) for value in values]


def on_chip(*values):
    return [pltpu.with_memory_space_constraint(value, pltpu.VMEM) for value in values]


def call(body, out_shape, in_specs, scratch, flops, moved, limit):
    return pl.pallas_call(
        body,
        out_shape=out_shape,
        in_specs=in_specs,
        out_specs=jax.tree.map(lambda _: VMEM, out_shape),
        scratch_shapes=scratch,
        compiler_params=pltpu.CompilerParams(vmem_limit_bytes=limit),
        cost_estimate=pl.CostEstimate(flops=flops, bytes_accessed=moved, transcendentals=0),
    )


def exchange(blocks):
    return lax.all_to_all(blocks, "wide", split_axis=0, concat_axis=0, tiled=True)


def own_half(ref):
    half = ref.shape[1] // 2
    return pl.ds(pl.multiple_of(lax.rem(lax.axis_index("wide"), 2) * half, half), half)


def other_half(ref):
    half = ref.shape[1] // 2
    return pl.ds(pl.multiple_of((1 - lax.rem(lax.axis_index("wide"), 2)) * half, half), half)


def swap(value):
    devices = lax.axis_size("wide")
    return lax.ppermute(value, "wide", [(at, at ^ 1) for at in range(devices)])


def unfold(row_ref, held):
    held[...] = row_ref[...].astype(jnp.float32).reshape(held.shape)


def attention(
    query_ref, key_ref, value_ref, gate_ref, norm_ref, decay_ref, state_ref,
    ids_ref, weights_ref, w_out_ref, out_ref, coef_ref, w_out_half,
    rows, norm_held, decay_held, states, ids_held, weights_held,
    q_held, k_held, v_held, g_held, att, q_wide, sems,
):
    heads = decay_held.shape[0]
    block = heads // HEAD_BLOCKS
    started = []

    def fetch(source, target):
        copy = pltpu.make_async_copy(source, target, sems.at[len(started)])
        copy.start()
        started.append(copy)
        return copy

    small = [fetch(ref, rows.at[at]) for at, ref in enumerate((query_ref, key_ref))]
    small.append(fetch(decay_ref, decay_held))
    parts = [pl.ds(at * block, block) for at in range(HEAD_BLOCKS)]
    read = [fetch(state_ref.at[0, part], states.at[part]) for part in parts]
    later = [fetch(ref, rows.at[2 + at]) for at, ref in enumerate((value_ref, gate_ref))]
    later.append(fetch(norm_ref, norm_held))
    later.append(fetch(ids_ref, ids_held))
    later.append(fetch(weights_ref, weights_held))
    last = [fetch(w_out_ref.at[:, own_half(w_out_ref)], w_out_half)]

    for copy in small:
        copy.wait()
    unfold(rows.at[0], q_held)
    unfold(rows.at[1], k_held)
    q_rows = q_held[...]
    q_columns = q_rows.T
    both = jnp.sum(q_rows * k_held[...], axis=1, keepdims=True)
    for head in range(heads):
        q_wide[head] = jnp.broadcast_to(q_columns[:, head : head + 1], q_wide.shape[1:])
    for at in range(HEAD_BLOCKS):
        read[at].wait()
        for head in range(at * block, (at + 1) * block):
            seen = jnp.sum(q_wide[head] * states[head], axis=0, keepdims=True)
            fade = jnp.exp(jnp.full((1, LANES), -decay_held[head], jnp.float32))
            att[head : head + 1, :] = fade * seen
    for copy in later:
        copy.wait()
    unfold(rows.at[2], v_held)
    unfold(rows.at[3], g_held)
    found = att[...] + both * v_held[...]
    scale = lax.rsqrt(jnp.sum(found * found, keepdims=True) / found.size + 1e-06)
    out_ref[...] = found * scale * norm_held[...] * jax.nn.sigmoid(g_held[...])

    owner = lax.axis_index("wide") // SPLIT
    named = jnp.where(ids_held[...] == owner, weights_held[...], 0.0)
    along = jnp.sum(named, axis=0, keepdims=True)
    square = (coef_ref.shape[0], coef_ref.shape[0])
    same = lax.broadcasted_iota(jnp.int32, square, 0) == lax.broadcasted_iota(jnp.int32, square, 1)
    column = jnp.sum(jnp.where(same, along, 0.0), axis=1, keepdims=True)
    coef_ref[...] = jnp.broadcast_to(column, coef_ref.shape)
    for copy in last:
        copy.wait()


def pair_up(rows_ref, _gate_ref, _up_ref, _down_ref, out_ref):
    heads = rows_ref.shape[0]
    if out_ref.shape[0] == heads:
        out_ref[...] = rows_ref[...]
        return
    for core in range(2):
        of_core = rows_ref[pl.ds(core, heads // 2, stride=2), :]
        out_ref[pl.ds(core, heads // 2, stride=4), :] = of_core
        out_ref[pl.ds(core + 2, heads // 2, stride=4), :] = of_core


def columns_to_blocks(made, spread, out_ref):
    rows, groups, size, _ = out_ref.shape
    tiles = groups * size
    for tile in range(tiles):
        spread[pl.ds(tile, rows, stride=tiles), :] = made[:, tile * LANES : (tile + 1) * LANES]
    for row in range(rows):
        for group in range(groups):
            lines = spread[pl.ds(row * tiles + group * size, size), :]
            out_ref[row, group] = lines.astype(out_ref.dtype)


def blocks_to_columns(blocks_ref, spread, inputs):
    rows, groups, size, _ = blocks_ref.shape
    tiles = groups * size
    for row in range(rows):
        for group in range(groups):
            lines = pl.ds(row * tiles + group * size, size)
            spread[lines, :] = blocks_ref[row, group].astype(jnp.float32)
    for tile in range(tiles):
        inputs[:, tile * LANES : (tile + 1) * LANES] = spread[
            pl.ds(tile, rows, stride=tiles), :
        ].astype(jnp.bfloat16)
    return inputs[...]


def multiply(left, right):
    return jnp.dot(left, right, preferred_element_type=jnp.float32)


def by_rows(left, weight):
    return lax.dot_general(
        left, weight, (((1,), (1,)), ((), ())), preferred_element_type=jnp.float32
    )


def project(*refs):
    *column_refs, w_ref, w_other_ref, _up_ref, _down_ref, _gate_ref, out_ref, spread = refs
    rows = out_ref.shape[0]
    if len(column_refs) == 1:
        pair = [column_refs[0][pl.ds(core, rows, stride=2), :] for core in range(2)]
    else:
        pair = [ref[...] for ref in column_refs]
    first = lax.rem(lax.axis_index("wide"), 2) == 0
    own = jnp.where(first, pair[0], pair[1]).astype(jnp.bfloat16)
    other = jnp.where(first, pair[1], pair[0]).astype(jnp.bfloat16)
    made = multiply(own, w_ref[...]) + multiply(other, w_other_ref[:, own_half(w_other_ref)])
    columns_to_blocks(made, spread, out_ref)


def add_up(parts_ref, held):
    devices, groups, size, _ = parts_ref.shape
    for half in range(2):
        total = parts_ref[half].astype(jnp.float32)
        for at in range(half + 2, devices, 2):
            total = total + parts_ref[at].astype(jnp.float32)
        for group in range(groups):
            start = (half * groups + group) * size
            held[start : start + size, :] = total[group]


def middle(parts_ref, resid_ref, gain_ref, _up_ref, _down_ref, _gate_ref, hid_ref, copies_ref, held, resid_rows):
    devices, groups, size, _ = copies_ref.shape
    add_up(parts_ref, held)
    unfold(resid_ref, resid_rows)
    hid = (resid_rows[...] + held[...]).astype(jnp.bfloat16).astype(jnp.float32)
    hid_ref[...] = hid
    scale = lax.rsqrt(jnp.sum(hid * hid, keepdims=True) / hid.size + 1e-06)
    held[...] = hid * scale * gain_ref[...]
    for half in range(2):
        for group in range(groups):
            start = (half * groups + group) * size
            lines = held[start : start + size, :].astype(jnp.bfloat16)
            for at in range(half, devices, 2):
                copies_ref[at, group] = lines


def experts_own(blocks_ref, gate_ref, up_ref, gate_out, up_out, spread, inputs):
    given = blocks_to_columns(blocks_ref, spread, inputs)
    gate_out[...] = by_rows(given, gate_ref[:, own_half(gate_ref)])
    up_out[...] = by_rows(given, up_ref[:, own_half(up_ref)])


def experts_other(
    blocks_ref, gate_ref, up_ref, down_ref, gate_held, up_held, coef_ref,
    inner_ref, send_ref, spread, inputs,
):
    given = blocks_to_columns(blocks_ref, spread, inputs)
    gate = gate_held[...] + by_rows(given, gate_ref[:, other_half(gate_ref)])
    upper = up_held[...] + by_rows(given, up_ref[:, other_half(up_ref)])
    inner = (jax.nn.silu(gate) * upper).astype(jnp.bfloat16)
    inner_ref[...] = inner
    made = multiply(inner, down_ref[:, other_half(down_ref)])
    coef = coef_ref[...]
    for at in range(0, made.shape[1], LANES):
        send_ref[:, at : at + LANES] = (made[:, at : at + LANES] * coef).astype(send_ref.dtype)


def experts_last(inner_ref, coef_ref, down_ref, out_ref):
    made = multiply(inner_ref[...], down_ref[:, own_half(down_ref)])
    coef = coef_ref[...]
    for at in range(0, made.shape[1], LANES):
        out_ref[:, at : at + LANES] = made[:, at : at + LANES] * coef


def join(own_ref, other_ref, out_ref, spread):
    columns_to_blocks(own_ref[...] + other_ref[...].astype(jnp.float32), spread, out_ref)


def finish(parts_ref, hid_ref, out_ref, held):
    add_up(parts_ref, held)
    held[...] = hid_ref[...] + held[...]
    for at in range(held.shape[0]):
        out_ref[0:1, at * LANES : (at + 1) * LANES] = held[at : at + 1, :].astype(out_ref.dtype)


def shards(
    resid,
    query,
    key,
    value,
    state,
    decay,
    out_gate,
    norm_gain,
    w_out,
    moe_gain,
    w_gate,
    w_up,
    w_down,
    expert_ids,
    expert_weights,
):
    width = resid.shape[1]
    half = width // 2
    heads = decay.shape[0]
    features = query.shape[1]
    devices = lax.axis_size("wide")
    each = features // devices
    tiles = width // LANES
    hidden = w_gate.shape[1]
    size = next(size for size in (8, 4, 2, 1) if tiles // 2 % size == 0)
    f32, bf16 = jnp.float32, jnp.bfloat16
    row = pltpu.VMEM((tiles, LANES), f32)
    blocks = pltpu.VMEM((devices, tiles // 2 // size, size, LANES), bf16)
    spread = pltpu.VMEM((devices * tiles // 2, LANES), f32)
    per_head = pltpu.VMEM((heads, LANES), f32)
    paired = each == LANES

    attn, coef, w_out_half = call(
        attention,
        (
            per_head,
            pltpu.VMEM((devices, LANES), f32),
            pltpu.VMEM((each, half), bf16),
        ),
        [HBM] * 10,
        [
            pltpu.VMEM((4, 1, features), bf16),
            per_head,
            pltpu.SMEM((heads,), f32),
            pltpu.VMEM(state.shape[1:], f32),
            pltpu.VMEM((2, devices), jnp.int32),
            pltpu.VMEM((2, devices), f32),
        ]
        + [per_head] * 5
        + [pltpu.VMEM(state.shape[1:], f32)]
        + [pltpu.SemaphoreType.DMA((9 + HEAD_BLOCKS,))],
        2 * state.size,
        4 * state.size,
        8 * MIB,
    )(
        *off_chip(
            query,
            key,
            value,
            out_gate,
            norm_gain.reshape(heads, LANES),
            decay,
            state,
            expert_ids.T,
            expert_weights.T,
            w_out,
        )
    )
    w_out_other = swap(w_out)
    w_gate, w_up, w_down = (w.reshape(w.shape[1:]) for w in (w_gate, w_up, w_down))
    attn = call(
        pair_up,
        pltpu.VMEM((2 * heads if paired else heads, LANES), f32),
        [VMEM] + [HBM] * 3,
        [],
        heads * LANES,
        8 * heads * LANES,
        2 * MIB,
    )(*on_chip(attn), *off_chip(w_gate, w_up, w_down))
    if paired:
        columns = exchange(attn.reshape(devices, 2, LANES))
        columns = [columns.reshape(2 * devices, LANES)]
    else:
        attn = jnp.repeat(attn.reshape(devices // 2, 2, each), 2, axis=0)
        columns = exchange(attn)
        columns = [columns[:, core] for core in range(2)]
    parts = call(
        project,
        blocks,
        [VMEM] * (5 + len(columns)),
        [spread],
        2 * devices * w_out.size,
        2 * w_out.size,
        4 * MIB,
    )(*on_chip(*columns, w_out_half, w_out_other, w_up, w_down, w_gate))
    hid, copies = call(
        middle, (row, blocks), [VMEM] * 6, [row, row], devices * width, 4 * devices * width, 2 * MIB
    )(*on_chip(exchange(parts), resid, moe_gain.reshape(tiles, LANES), w_up, w_down, w_gate))
    given = exchange(copies)
    given_other = swap(given)
    inputs = pltpu.VMEM((devices, half), bf16)
    partial_sum = pltpu.VMEM((devices, hidden), f32)
    sums = call(
        experts_own,
        (partial_sum, partial_sum),
        [VMEM] * 3,
        [spread, inputs],
        2 * devices * hidden * width,
        4 * hidden * width,
        8 * MIB,
    )(*on_chip(given, w_gate, w_up))
    inner, send = call(
        experts_other,
        (pltpu.VMEM((devices, hidden), bf16), inputs),
        [VMEM] * 7,
        [spread, inputs],
        3 * devices * hidden * width,
        4 * hidden * width,
        8 * MIB,
    )(*on_chip(given_other, w_gate, w_up, w_down, *sums, coef))
    received = swap(send)
    own = call(
        experts_last,
        pltpu.VMEM((devices, half), f32),
        [VMEM] * 3,
        [],
        devices * hidden * width,
        hidden * width,
        4 * MIB,
    )(*on_chip(inner, coef, w_down))
    outcome = call(
        join, blocks, [VMEM] * 2, [spread], devices * width, 4 * devices * width, 4 * MIB
    )(*on_chip(own, received))
    return call(
        finish,
        jax.ShapeDtypeStruct((1, width), bf16),
        [VMEM, VMEM],
        [row],
        devices * width,
        2 * devices * width,
        2 * MIB,
    )(*on_chip(exchange(outcome), hid))


def solution(mesh):
    return jax.shard_map(
        shards,
        mesh=mesh,
        in_specs=(
            P(("group", "wide"), None),
            P(("group", "wide"), None),
            P(("group", "wide"), None),
            P(("group", "wide"), None),
            P(("group", "wide"), None, None, None),
            P(),
            P(("group", "wide"), None),
            P(),
            P("wide", None),
            P(),
            P("wide", None, None),
            P("wide", None, None),
            P("wide", None, None),
            P("group", None),
            P("group", None),
        ),
        out_specs=P(("group", "wide"), None),
        check_vma=False,
    )
```

```python
import jax
import jax.numpy as jnp
from jax import lax
from jax.experimental import pallas as pl
from jax.experimental.pallas import tpu as pltpu
from jax.sharding import PartitionSpec as P

SPLIT = 8
LANES = 128
HEAD_BLOCKS = 4
VMEM = pl.BlockSpec(memory_space=pltpu.VMEM)
HBM = pl.BlockSpec(memory_space=pltpu.HBM)
MIB = 1024 * 1024


def off_chip(*values):
    return [pltpu.with_memory_space_constraint(value, pltpu.HBM) for value in values]


def on_chip(*values):
    return [pltpu.with_memory_space_constraint(value, pltpu.VMEM) for value in values]


def call(body, out_shape, in_specs, scratch, flops, moved, limit):
    return pl.pallas_call(
        body,
        out_shape=out_shape,
        in_specs=in_specs,
        out_specs=jax.tree.map(lambda _: VMEM, out_shape),
        scratch_shapes=scratch,
        compiler_params=pltpu.CompilerParams(vmem_limit_bytes=limit),
        cost_estimate=pl.CostEstimate(flops=flops, bytes_accessed=moved, transcendentals=0),
    )


def exchange(blocks):
    return lax.all_to_all(blocks, "wide", split_axis=0, concat_axis=0, tiled=True)


def own_half(ref):
    half = ref.shape[1] // 2
    return pl.ds(pl.multiple_of(lax.rem(lax.axis_index("wide"), 2) * half, half), half)


def other_half(ref):
    half = ref.shape[1] // 2
    return pl.ds(pl.multiple_of((1 - lax.rem(lax.axis_index("wide"), 2)) * half, half), half)


def swap(value):
    devices = lax.axis_size("wide")
    return lax.ppermute(value, "wide", [(at, at ^ 1) for at in range(devices)])


def unfold(row_ref, held):
    held[...] = row_ref[...].astype(jnp.float32).reshape(held.shape)


def attention(
    query_ref, key_ref, value_ref, gate_ref, norm_ref, decay_ref, state_ref,
    ids_ref, weights_ref, out_ref, coef_ref,
    rows, norm_held, decay_held, states, ids_held, weights_held,
    q_held, k_held, v_held, g_held, att, q_wide, sems,
):
    heads = decay_held.shape[0]
    block = heads // HEAD_BLOCKS
    started = []

    def fetch(source, target):
        copy = pltpu.make_async_copy(source, target, sems.at[len(started)])
        copy.start()
        started.append(copy)
        return copy

    small = [fetch(ref, rows.at[at]) for at, ref in enumerate((query_ref, key_ref))]
    small.append(fetch(decay_ref, decay_held))
    parts = [pl.ds(at * block, block) for at in range(HEAD_BLOCKS)]
    read = [fetch(state_ref.at[0, part], states.at[part]) for part in parts]
    later = [fetch(ref, rows.at[2 + at]) for at, ref in enumerate((value_ref, gate_ref))]
    later.append(fetch(norm_ref, norm_held))
    later.append(fetch(ids_ref, ids_held))
    later.append(fetch(weights_ref, weights_held))

    for copy in small:
        copy.wait()
    unfold(rows.at[0], q_held)
    unfold(rows.at[1], k_held)
    q_rows = q_held[...]
    q_columns = q_rows.T
    both = jnp.sum(q_rows * k_held[...], axis=1, keepdims=True)
    for head in range(heads):
        q_wide[head] = jnp.broadcast_to(q_columns[:, head : head + 1], q_wide.shape[1:])
    for at in range(HEAD_BLOCKS):
        read[at].wait()
        for head in range(at * block, (at + 1) * block):
            seen = jnp.sum(q_wide[head] * states[head], axis=0, keepdims=True)
            fade = jnp.exp(jnp.full((1, LANES), -decay_held[head], jnp.float32))
            att[head : head + 1, :] = fade * seen
    for copy in later:
        copy.wait()
    unfold(rows.at[2], v_held)
    unfold(rows.at[3], g_held)
    found = att[...] + both * v_held[...]
    scale = lax.rsqrt(jnp.sum(found * found, keepdims=True) / found.size + 1e-06)
    out_ref[...] = found * scale * norm_held[...] * jax.nn.sigmoid(g_held[...])

    owner = lax.axis_index("wide") // SPLIT
    named = jnp.where(ids_held[...] == owner, weights_held[...], 0.0)
    along = jnp.sum(named, axis=0, keepdims=True)
    square = (coef_ref.shape[0], coef_ref.shape[0])
    same = lax.broadcasted_iota(jnp.int32, square, 0) == lax.broadcasted_iota(jnp.int32, square, 1)
    column = jnp.sum(jnp.where(same, along, 0.0), axis=1, keepdims=True)
    coef_ref[...] = jnp.broadcast_to(column, coef_ref.shape)


def pair_up(rows_ref, _out_ref, _gate_ref, _up_ref, _down_ref, out_ref):
    heads = rows_ref.shape[0]
    if out_ref.shape[0] == heads:
        out_ref[...] = rows_ref[...]
        return
    for core in range(2):
        of_core = rows_ref[pl.ds(core, heads // 2, stride=2), :]
        out_ref[pl.ds(core, heads // 2, stride=4), :] = of_core
        out_ref[pl.ds(core + 2, heads // 2, stride=4), :] = of_core


def columns_to_blocks(made, spread, out_ref):
    rows, groups, size, _ = out_ref.shape
    tiles = groups * size
    for tile in range(tiles):
        spread[pl.ds(tile, rows, stride=tiles), :] = made[:, tile * LANES : (tile + 1) * LANES]
    for row in range(rows):
        for group in range(groups):
            lines = spread[pl.ds(row * tiles + group * size, size), :]
            out_ref[row, group] = lines.astype(out_ref.dtype)


def blocks_to_columns(blocks_ref, spread, inputs):
    rows, groups, size, _ = blocks_ref.shape
    tiles = groups * size
    for row in range(rows):
        for group in range(groups):
            lines = pl.ds(row * tiles + group * size, size)
            spread[lines, :] = blocks_ref[row, group].astype(jnp.float32)
    for tile in range(tiles):
        inputs[:, tile * LANES : (tile + 1) * LANES] = spread[
            pl.ds(tile, rows, stride=tiles), :
        ].astype(jnp.bfloat16)
    return inputs[...]


def multiply(left, right):
    return jnp.dot(left, right, preferred_element_type=jnp.float32)


def by_rows(left, weight):
    return lax.dot_general(
        left, weight, (((1,), (1,)), ((), ())), preferred_element_type=jnp.float32
    )


def project(*refs):
    *column_refs, w_ref, w_other_ref, _up_ref, _down_ref, _gate_ref, out_ref, spread = refs
    rows = out_ref.shape[0]
    if len(column_refs) == 1:
        pair = [column_refs[0][pl.ds(core, rows, stride=2), :] for core in range(2)]
    else:
        pair = [ref[...] for ref in column_refs]
    first = lax.rem(lax.axis_index("wide"), 2) == 0
    own = jnp.where(first, pair[0], pair[1]).astype(jnp.bfloat16)
    other = jnp.where(first, pair[1], pair[0]).astype(jnp.bfloat16)
    made = multiply(own, w_ref[:, own_half(w_ref)]) + multiply(other, w_other_ref[:, own_half(w_other_ref)])
    columns_to_blocks(made, spread, out_ref)


def add_up(parts_ref, held):
    devices, groups, size, _ = parts_ref.shape
    for half in range(2):
        total = parts_ref[half].astype(jnp.float32)
        for at in range(half + 2, devices, 2):
            total = total + parts_ref[at].astype(jnp.float32)
        for group in range(groups):
            start = (half * groups + group) * size
            held[start : start + size, :] = total[group]


def middle(parts_ref, resid_ref, gain_ref, _up_ref, _down_ref, _gate_ref, hid_ref, copies_ref, held, resid_rows):
    devices, groups, size, _ = copies_ref.shape
    add_up(parts_ref, held)
    unfold(resid_ref, resid_rows)
    hid = (resid_rows[...] + held[...]).astype(jnp.bfloat16).astype(jnp.float32)
    hid_ref[...] = hid
    scale = lax.rsqrt(jnp.sum(hid * hid, keepdims=True) / hid.size + 1e-06)
    held[...] = hid * scale * gain_ref[...]
    for half in range(2):
        for group in range(groups):
            start = (half * groups + group) * size
            lines = held[start : start + size, :].astype(jnp.bfloat16)
            for at in range(half, devices, 2):
                copies_ref[at, group] = lines


def experts_own(blocks_ref, gate_ref, up_ref, gate_out, up_out, spread, inputs):
    given = blocks_to_columns(blocks_ref, spread, inputs)
    gate_out[...] = by_rows(given, gate_ref[:, own_half(gate_ref)])
    up_out[...] = by_rows(given, up_ref[:, own_half(up_ref)])


def experts_other(
    blocks_ref, gate_ref, up_ref, down_ref, gate_held, up_held, coef_ref,
    inner_ref, send_ref, spread, inputs,
):
    given = blocks_to_columns(blocks_ref, spread, inputs)
    gate = gate_held[...] + by_rows(given, gate_ref[:, other_half(gate_ref)])
    upper = up_held[...] + by_rows(given, up_ref[:, other_half(up_ref)])
    inner = (jax.nn.silu(gate) * upper).astype(jnp.bfloat16)
    inner_ref[...] = inner
    made = multiply(inner, down_ref[:, other_half(down_ref)])
    coef = coef_ref[...]
    for at in range(0, made.shape[1], LANES):
        send_ref[:, at : at + LANES] = (made[:, at : at + LANES] * coef).astype(send_ref.dtype)


def experts_last(inner_ref, coef_ref, down_ref, out_ref):
    made = multiply(inner_ref[...], down_ref[:, own_half(down_ref)])
    coef = coef_ref[...]
    for at in range(0, made.shape[1], LANES):
        out_ref[:, at : at + LANES] = made[:, at : at + LANES] * coef


def join(own_ref, other_ref, out_ref, spread):
    columns_to_blocks(own_ref[...] + other_ref[...].astype(jnp.float32), spread, out_ref)


def finish(parts_ref, hid_ref, out_ref, held):
    add_up(parts_ref, held)
    held[...] = hid_ref[...] + held[...]
    for at in range(held.shape[0]):
        out_ref[0:1, at * LANES : (at + 1) * LANES] = held[at : at + 1, :].astype(out_ref.dtype)


def shards(
    resid,
    query,
    key,
    value,
    state,
    decay,
    out_gate,
    norm_gain,
    w_out,
    moe_gain,
    w_gate,
    w_up,
    w_down,
    expert_ids,
    expert_weights,
):
    width = resid.shape[1]
    half = width // 2
    heads = decay.shape[0]
    features = query.shape[1]
    devices = lax.axis_size("wide")
    each = features // devices
    tiles = width // LANES
    hidden = w_gate.shape[1]
    size = next(size for size in (8, 4, 2, 1) if tiles // 2 % size == 0)
    f32, bf16 = jnp.float32, jnp.bfloat16
    row = pltpu.VMEM((tiles, LANES), f32)
    blocks = pltpu.VMEM((devices, tiles // 2 // size, size, LANES), bf16)
    spread = pltpu.VMEM((devices * tiles // 2, LANES), f32)
    per_head = pltpu.VMEM((heads, LANES), f32)
    paired = each == LANES

    attn, coef = call(
        attention,
        (
            per_head,
            pltpu.VMEM((devices, LANES), f32),
        ),
        [HBM] * 9,
        [
            pltpu.VMEM((4, 1, features), bf16),
            per_head,
            pltpu.SMEM((heads,), f32),
            pltpu.VMEM(state.shape[1:], f32),
            pltpu.VMEM((2, devices), jnp.int32),
            pltpu.VMEM((2, devices), f32),
        ]
        + [per_head] * 5
        + [pltpu.VMEM(state.shape[1:], f32)]
        + [pltpu.SemaphoreType.DMA((8 + HEAD_BLOCKS,))],
        2 * state.size,
        4 * state.size,
        8 * MIB,
    )(
        *off_chip(
            query,
            key,
            value,
            out_gate,
            norm_gain.reshape(heads, LANES),
            decay,
            state,
            expert_ids.T,
            expert_weights.T,
        )
    )
    w_out_other = swap(w_out)
    w_gate, w_up, w_down = (w.reshape(w.shape[1:]) for w in (w_gate, w_up, w_down))
    attn = call(
        pair_up,
        pltpu.VMEM((2 * heads if paired else heads, LANES), f32),
        [VMEM] + [HBM] * 4,
        [],
        heads * LANES,
        8 * heads * LANES,
        2 * MIB,
    )(*on_chip(attn), *off_chip(w_out, w_gate, w_up, w_down))
    if paired:
        columns = exchange(attn.reshape(devices, 2, LANES))
        columns = [columns.reshape(2 * devices, LANES)]
    else:
        attn = jnp.repeat(attn.reshape(devices // 2, 2, each), 2, axis=0)
        columns = exchange(attn)
        columns = [columns[:, core] for core in range(2)]
    parts = call(
        project,
        blocks,
        [VMEM] * (5 + len(columns)),
        [spread],
        2 * devices * w_out.size,
        2 * w_out.size,
        4 * MIB,
    )(*on_chip(*columns, w_out, w_out_other, w_up, w_down, w_gate))
    hid, copies = call(
        middle, (row, blocks), [VMEM] * 6, [row, row], devices * width, 4 * devices * width, 2 * MIB
    )(*on_chip(exchange(parts), resid, moe_gain.reshape(tiles, LANES), w_up, w_down, w_gate))
    given = exchange(copies)
    given_other = swap(given)
    inputs = pltpu.VMEM((devices, half), bf16)
    partial_sum = pltpu.VMEM((devices, hidden), f32)
    sums = call(
        experts_own,
        (partial_sum, partial_sum),
        [VMEM] * 3,
        [spread, inputs],
        2 * devices * hidden * width,
        4 * hidden * width,
        8 * MIB,
    )(*on_chip(given, w_gate, w_up))
    inner, send = call(
        experts_other,
        (pltpu.VMEM((devices, hidden), bf16), inputs),
        [VMEM] * 7,
        [spread, inputs],
        3 * devices * hidden * width,
        4 * hidden * width,
        8 * MIB,
    )(*on_chip(given_other, w_gate, w_up, w_down, *sums, coef))
    received = swap(send)
    own = call(
        experts_last,
        pltpu.VMEM((devices, half), f32),
        [VMEM] * 3,
        [],
        devices * hidden * width,
        hidden * width,
        4 * MIB,
    )(*on_chip(inner, coef, w_down))
    outcome = call(
        join, blocks, [VMEM] * 2, [spread], devices * width, 4 * devices * width, 4 * MIB
    )(*on_chip(own, received))
    return call(
        finish,
        jax.ShapeDtypeStruct((1, width), bf16),
        [VMEM, VMEM],
        [row],
        devices * width,
        2 * devices * width,
        2 * MIB,
    )(*on_chip(exchange(outcome), hid))


def solution(mesh):
    return jax.shard_map(
        shards,
        mesh=mesh,
        in_specs=(
            P(("group", "wide"), None),
            P(("group", "wide"), None),
            P(("group", "wide"), None),
            P(("group", "wide"), None),
            P(("group", "wide"), None, None, None),
            P(),
            P(("group", "wide"), None),
            P(),
            P("wide", None),
            P(),
            P("wide", None, None),
            P("wide", None, None),
            P("wide", None, None),
            P("group", None),
            P("group", None),
        ),
        out_specs=P(("group", "wide"), None),
        check_vma=False,
    )
```
